512 devices in a mesh: sec: 2 (over z_hi), gx: 32 (over z_lo, x), row: 8 (over y, core).
Axes of the slice: x: 4, y: 4, z: 16 (z_hi: 2, z_lo: 8; z = z_hi * 8 + z_lo), core: 2. Of those that a mesh axis runs over, the one named last changes fastest.
Arguments:
- fields: float32 [2, 5, 256, 64, 128], P('sec', None, 'gx', 'row'), may hold values from -1.25 to 5, as said below
- mean_flow: float32 [5, 256, 64, 128], P(None, 'gx', 'row'), may hold values from -1 to 1.4, as said below
- source_blocks: int32 [64], replicated, may hold values 0 or 1
Outputs:
- fields_out: float32 [2, 5, 256, 64, 128], P('sec', None, 'gx', 'row')
The draws below stay inside these ranges and needn't reach their ends.
Inputs may be any that keep to these rules, and one draw needn't show every extreme that they name: `fields`: section 0 holds density in 0.8 to 1.25, momenta of velocities within -1 to 1 and total energy of a pressure in 0.8 to 1.25; section 1 holds perturbations within -1 to 1. `mean_flow`: mean velocities lie within -1 to 1, mean density in 0.8 to 1.25 and sound speed in 0.7 to 1.4.
All inputs are finite; a program needn't handle non-finite values.
Results may differ from the reference program's by a relative error of at most 0.0001.
Values sent between devices are 32-bit elements; how exact they have to be, the bound alone decides.
A program may use at most 64 MiB of HBM per device.

```python
import jax
import jax.numpy as jnp

CZ = 128
MBLEN = 4
STEPS = 1
NX = 256
NR = 64
BLOCKS = 64


GAMMA = 1.4


def draw_fields(key, part):
    subkeys = jax.random.split(key, 4)
    grid_shape = (NX, NR, CZ)
    density = jax.random.uniform(subkeys[0], grid_shape, jnp.float32, 0.8, 1.25)
    pressure = jax.random.uniform(subkeys[2], grid_shape, jnp.float32, 0.8, 1.25)
    velocity = jnp.clip(0.3 * jax.random.normal(subkeys[1], (3,) + grid_shape, jnp.float32), -1.0, 1.0)
    sound = jnp.clip(0.3 * jax.random.normal(subkeys[3], (5,) + grid_shape, jnp.float32), -1.0, 1.0)
    energy = pressure / (GAMMA - 1.0) + 0.5 * density * jnp.sum(velocity * velocity, axis=0)
    flow_part = jnp.concatenate([density[None], density[None] * velocity, energy[None]], axis=0)
    return jnp.stack([flow_part, sound])


def draw_mean_flow(key, part):
    subkeys = jax.random.split(jax.random.fold_in(key, 7), 3)
    grid_shape = (NX, NR, CZ)
    velocity = jnp.clip(0.3 * jax.random.normal(subkeys[0], (3,) + grid_shape, jnp.float32), -1.0, 1.0)
    density = jax.random.uniform(subkeys[1], grid_shape, jnp.float32, 0.8, 1.25)
    speed = jax.random.uniform(subkeys[2], grid_shape, jnp.float32, 0.7, 1.4)
    return jnp.concatenate([velocity, density[None], speed[None]], axis=0)


def set_ends(values, key, least, largest):
    longest = values.shape.index(max(values.shape))
    spots = []
    for shift in (0, 1):
        where = [jax.random.randint(jax.random.fold_in(key, axis), (), 0, length) for axis, length in enumerate(values.shape)]
        where[longest] = (where[longest] + shift) % values.shape[longest]
        spots.append(tuple(where))
    return values.at[spots[0]].set(least).at[spots[1]].set(largest)


def setup_inputs(seed: int = 0) -> dict:
    keys = jax.random.split(jax.random.key(seed), 4)
    return {
        "fields": draw_fields(jax.random.fold_in(keys[3], 71), 0),
        "mean_flow": draw_mean_flow(jax.random.fold_in(keys[3], 71), 0),
        "source_blocks": set_ends((jax.random.randint(keys[2], (BLOCKS,), 0, 4) < 3).astype(jnp.int32), jax.random.fold_in(keys[2], 1), 0, 1),
    }


GAMMA = 1.4
STEP_DT = 0.2
VISCOSITY = 0.05


def offset_cells(values, direction, shift_by):
    length_x = values.shape[-3]
    length_y = values.shape[-2]
    if direction == 2:
        return jnp.roll(values[..., 2:length_x - 2, 2:length_y - 2, :], -shift_by, axis=-1)
    if direction == 0:
        return values[..., 2 + shift_by:length_x - 2 + shift_by, 2:length_y - 2, :]
    return values[..., 2:length_x - 2, 2 + shift_by:length_y - 2 + shift_by, :]


def central_first(values, direction):
    return (8.0 * (offset_cells(values, direction, 1) - offset_cells(values, direction, -1))
            - (offset_cells(values, direction, 2) - offset_cells(values, direction, -2))) / 12.0


def central_second(values, direction):
    return (-offset_cells(values, direction, 2) + 16.0 * offset_cells(values, direction, 1)
            - 30.0 * offset_cells(values, direction, 0) + 16.0 * offset_cells(values, direction, -1)
            - offset_cells(values, direction, -2)) / 12.0


def trim_rim(values, amount):
    if amount == 0:
        return values
    return values[..., amount:-amount, amount:-amount, :]


def flow_rate(padded):
    density = padded[0]
    momentum = padded[1:4]
    energy = padded[4]
    velocity = momentum / density
    pressure = (GAMMA - 1.0) * (energy - 0.5 * jnp.sum(momentum * velocity, axis=0))
    total = None
    for direction in range(3):
        along = velocity[direction]
        unit_vector = jnp.zeros((3,), jnp.float32).at[direction].set(1.0)
        middle = momentum * along[None] + pressure[None] * unit_vector[:, None, None, None]
        flux = jnp.concatenate([momentum[direction][None], middle, ((energy + pressure) * along)[None]], axis=0)
        term = -central_first(flux, direction)
        total = term if total is None else total + term
    spread = central_second(padded, 0) + central_second(padded, 1) + central_second(padded, 2)
    return total + VISCOSITY * spread


def lamb_vector(velocity):
    interior = trim_rim(velocity, 2)
    spin_first = central_first(velocity[2], 1) - central_first(velocity[1], 2)
    spin_second = central_first(velocity[0], 2) - central_first(velocity[2], 0)
    spin_third = central_first(velocity[1], 0) - central_first(velocity[0], 1)
    return jnp.stack([spin_second * interior[2] - spin_third * interior[1],
                      spin_third * interior[0] - spin_first * interior[2],
                      spin_first * interior[1] - spin_second * interior[0]])


def acoustic_rate(padded, mean_here, source):
    mean_velocity = mean_here[0:3]

    def convect(values):
        return (mean_velocity[0] * central_first(values, 0) + mean_velocity[1] * central_first(values, 1)
                + mean_velocity[2] * central_first(values, 2))

    divergence = central_first(padded[1], 0) + central_first(padded[2], 1) + central_first(padded[3], 2)
    density_rate = -convect(padded[0]) - mean_here[3] * divergence
    velocity_rates = [-convect(padded[1 + component]) - central_first(padded[4], component) / mean_here[3]
                      - source[component] for component in range(3)]
    pressure_rate = -convect(padded[4]) - mean_here[3] * mean_here[4] * mean_here[4] * divergence
    return jnp.stack([density_rate] + velocity_rates + [pressure_rate])


def pad_wrap(values, width):
    return jnp.pad(values, ((0, 0), (width, width), (width, width), (0, 0)), mode="wrap")


def runge_kutta(state, rate_function):
    slope_one = rate_function(pad_wrap(state, 2))
    slope_two = rate_function(pad_wrap(state + 0.5 * STEP_DT * slope_one, 2))
    slope_three = rate_function(pad_wrap(state + 0.5 * STEP_DT * slope_two, 2))
    slope_four = rate_function(pad_wrap(state + STEP_DT * slope_three, 2))
    return state + (STEP_DT / 6.0) * (slope_one + 2.0 * slope_two + 2.0 * slope_three + slope_four)


def reference(fields, mean_flow, source_blocks):
    flow_state = fields[0]
    sound_state = fields[1]
    mask_rows = jnp.repeat(source_blocks.astype(jnp.float32), MBLEN)
    for step_index in range(STEPS):
        padded = pad_wrap(flow_state, 2)
        source = lamb_vector(padded[1:4] / padded[0]) * mask_rows[None, :, None, None]
        flow_state = runge_kutta(flow_state, flow_rate)
        sound_state = runge_kutta(sound_state, lambda values: acoustic_rate(values, mean_flow, source))
    return jnp.stack([flow_state, sound_state])
```

```python
import functools

import jax
import jax.numpy as jnp
from jax import lax
from jax.experimental import pallas as pl
from jax.experimental.pallas import tpu as pltpu
from jax.sharding import PartitionSpec as P

MESH = pl.DeviceIdType.MESH
MBLEN = 4
GAMMA = 1.4
STEP_DT = 0.2
VISCOSITY = 0.05

EX = 8
EY = 8
HY = 4
WX = 3 * EX
WY = EY + 2 * HY

DIRECTIONS = ((1, 0), (-1, 0), (1, 1), (1, -1), (-1, 1), (-1, -1), (0, 1), (0, -1))

FIELD, MEAN, SPEED, PARTNER, STAGE = 0, 8, 16, 24, 25
SEMAPHORES = 27


def whole_x(dx):
    source = pl.ds(0, EX)
    target = pl.ds({1: 0, 0: EX, -1: 2 * EX}[dx], EX)
    return source, target


def part_x(dx, width):
    source = pl.ds({1: EX - width, 0: 0, -1: 0}[dx], EX if dx == 0 else width)
    target = pl.ds({1: EX - width, 0: EX, -1: 2 * EX}[dx], EX if dx == 0 else width)
    return source, target


def part_y(dy, width):
    source = ({1: EY - width, 0: 0, -1: 0}[dy], EY if dy == 0 else width)
    target = ({1: HY - width, 0: HY, -1: HY + EY}[dy], EY if dy == 0 else width)
    return source, target


def shift(values, axis, by):
    size = values.shape[axis]
    return pltpu.roll(values, (-by) % size, axis)


def derivative(values, axis):
    once = shift(values, axis, 1) - shift(values, axis, -1)
    return 8.0 * once - (shift(once, axis, 1) + shift(once, axis, -1))


def derivative_x(ref, c, x):
    return 8.0 * (ref[c, x + 1] - ref[c, x - 1]) - (ref[c, x + 2] - ref[c, x - 2])


def primitives(q):
    inverse = 1.0 / q[0]
    u = [q[1 + j] * inverse for j in range(3)]
    p = (GAMMA - 1.0) * (q[4] - 0.5 * (q[1] * u[0] + q[2] * u[1] + q[3] * u[2]))
    return u, p


def flux(q, u, p, d):
    parts = [q[1 + d]]
    for j in range(3):
        part = q[1 + j] * u[d]
        parts.append(part + p if j == d else part)
    parts.append((q[4] + p) * u[d])
    return parts


def fluxes_x(q_ref, f_ref, low, high):
    def row(x, carry):
        q = [q_ref[c, x] for c in range(5)]
        u, p = primitives(q)
        f = flux(q, u, p, 0)
        for c in range(1, 5):
            f_ref[c - 1, x] = f[c]
        return carry

    lax.fori_loop(low, high, row, 0)


def flow_row(q_ref, f_ref, x):
    q = [q_ref[c, x] for c in range(5)]
    u, p = primitives(q)
    along_y = flux(q, u, p, 1)
    along_z = flux(q, u, p, 2)
    rates = []
    for c in range(5):
        f, fc = (q_ref, 1) if c == 0 else (f_ref, c - 1)
        total = 8.0 * (f[fc, x - 1] - f[fc, x + 1]) + (f[fc, x + 2] - f[fc, x - 2])
        total += (16.0 * VISCOSITY) * (q_ref[c, x + 1] + q_ref[c, x - 1])
        total -= VISCOSITY * (q_ref[c, x + 2] + q_ref[c, x - 2])
        total -= (90.0 * VISCOSITY) * q[c]
        near, far = ((16.0 * VISCOSITY) * q[c], VISCOSITY * q[c])
        for axis, parts in ((0, along_y), (1, along_z)):
            eight = 8.0 * parts[c]
            total += shift(near - eight, axis, 1) + shift(near + eight, axis, -1)
            total += shift(parts[c] - far, axis, 2) - shift(parts[c] + far, axis, -2)
        rates.append(total * (1.0 / 12.0))
    return rates


def sound_row(a_ref, mean_ref, x):
    mean = [mean_ref[c, x] for c in range(5)]
    speed = [mean[j] * (1.0 / 12.0) for j in range(3)]
    density = mean[3] * (1.0 / 12.0)
    inverse = (1.0 / 12.0) / mean[3]
    slopes, carried = [], []
    for c in range(5):
        value = a_ref[c, x]
        d = [derivative_x(a_ref, c, x), derivative(value, 0), derivative(value, 1)]
        slopes.append(d)
        carried.append(speed[0] * d[0] + speed[1] * d[1] + speed[2] * d[2])
    divergence = density * (slopes[1][0] + slopes[2][1] + slopes[3][2])
    rates = [-carried[0] - divergence]
    for j in range(3):
        rates.append(-carried[1 + j] - slopes[4][j] * inverse)
    rates.append(-carried[4] - mean[4] * mean[4] * divergence)
    return rates


def lamb_row(u_ref, x):
    u = [u_ref[c, x] for c in range(3)]
    spin = (
        derivative(u[2], 0) - derivative(u[1], 1),
        derivative(u[0], 1) - derivative_x(u_ref, 2, x),
        derivative_x(u_ref, 1, x) - derivative(u[0], 0),
    )
    scale = 1.0 / 12.0
    return [
        scale * (spin[1] * u[2] - spin[2] * u[1]),
        scale * (spin[2] * u[0] - spin[0] * u[2]),
        scale * (spin[0] * u[1] - spin[1] * u[0]),
    ]


def kernel(
    nx,
    nr,
    fields,
    mean_flow,
    blocks,
    out,
    own,
    own_mean,
    own_speed,
    start,
    mean,
    speed,
    source,
    odd,
    even,
    flux_x,
    slope,
    send,
    receive,
    local,
):
    sec = lax.axis_index("sec")
    gx = lax.axis_index("gx")
    row = lax.axis_index("row")
    is_flow = sec == 0
    is_sound = sec == 1
    first, last = gx == 0, gx == nx - 1

    def place(section, dx, dy):
        return {
            "sec": section,
            "gx": lax.rem(gx + dx + nx, nx),
            "row": lax.rem(row + dy + nr, nr),
        }

    barrier = pltpu.get_barrier_semaphore()

    def greet(device):
        pl.semaphore_signal(barrier, inc=1, device_id=device, device_id_type=MESH)

    greet(place(1 - sec, 0, 0))
    for dx, dy in DIRECTIONS:
        greet(place(sec, dx, dy))
    for edge, dx in ((first, -1), (last, 1)):

        @pl.when(edge)
        def _():
            for dy in (-1, 0, 1):
                greet(place(1 - sec, dx, dy))

    inner_x, inner_y = pl.ds(EX, EX), pl.ds(HY, EY)
    load = pltpu.make_async_copy(fields.at[0], own, local.at[0])
    load.start()
    load_start = pltpu.make_async_copy(fields.at[0], start.at[:, inner_x, inner_y], local.at[1])
    load_start.start()
    load_mean = pltpu.make_async_copy(mean_flow, own_mean, local.at[2])
    load_inner = pltpu.make_async_copy(mean_flow, mean.at[:, inner_x, inner_y], local.at[3])

    @pl.when(is_sound)
    def _():
        load_mean.start()
        load_inner.start()

    load.wait()

    @pl.when(is_flow)
    def _():
        for x in range(EX):
            inverse = 1.0 / own[0, x]
            for j in range(3):
                own_speed[j, x] = own[1 + j, x] * inverse

    @pl.when(is_sound)
    def _():
        load_mean.wait()

    @pl.when(first | last)
    def _():
        pl.semaphore_wait(barrier, 12)

    @pl.when((gx > 0) & (gx < nx - 1))
    def _():
        pl.semaphore_wait(barrier, 9)

    def remote(origin, target, index, device):
        return pltpu.make_async_remote_copy(
            src_ref=origin,
            dst_ref=target,
            send_sem=send.at[index],
            recv_sem=receive.at[index],
            device_id=device,
            device_id_type=MESH,
        )

    def field_copy(i):
        dx, dy = DIRECTIONS[i]
        (sx, tx), (sy, ty) = whole_x(dx), part_y(dy, HY)
        return remote(
            own.at[:, sx, pl.ds(*sy)], start.at[:, tx, pl.ds(*ty)], FIELD + i, place(sec, dx, dy)
        )

    def mean_copy(i):
        dx, dy = DIRECTIONS[i]
        (sx, tx), (sy, ty) = part_x(dx, EX - 2), part_y(dy, HY - 2)
        return remote(
            own_mean.at[:, sx, pl.ds(*sy)], mean.at[:, tx, pl.ds(*ty)], MEAN + i, place(sec, dx, dy)
        )

    def speed_copy(i):
        dx, dy = DIRECTIONS[i]
        (_, tx), (sy, ty) = whole_x(dx), part_y(dy, HY)
        return remote(
            speed.at[:, inner_x, pl.ds(HY + sy[0], sy[1])],
            speed.at[:, tx, pl.ds(*ty)],
            SPEED + i,
            place(1, dx, dy),
        )

    def speed_around(i):
        dx, dy = DIRECTIONS[i]
        (sx, tx), (sy, ty) = whole_x(dx), part_y(dy, HY)
        return remote(
            own_speed.at[:, sx, pl.ds(*sy)],
            speed.at[:, tx, pl.ds(*ty)],
            SPEED + i,
            place(1, dx, dy),
        )

    partner_copy = remote(own_speed, speed.at[:, inner_x, inner_y], PARTNER, place(1, 0, 0))
    up = [i for i, d in enumerate(DIRECTIONS) if d[0] == 1]
    down = [i for i, d in enumerate(DIRECTIONS) if d[0] == -1]
    level = [i for i, d in enumerate(DIRECTIONS) if d[0] == 0]
    every = range(len(DIRECTIONS))

    @pl.when(is_flow)
    def _():
        partner_copy.start()

    for i in every:
        field_copy(i).start()

    @pl.when(is_flow & last)
    def _():
        for i in up:
            speed_around(i).start()

    @pl.when(is_flow & first)
    def _():
        for i in down:
            speed_around(i).start()

    @pl.when(is_sound)
    def _():
        for i in every:
            mean_copy(i).start()

    def stage_copies(ref):
        rows = pl.ds(4, WX - 8)
        return [
            remote(
                ref.at[:, rows, pl.ds(HY + EY - HY, HY)],
                ref.at[:, rows, pl.ds(0, HY)],
                STAGE,
                place(sec, 0, 1),
            ),
            remote(
                ref.at[:, rows, pl.ds(HY, HY)],
                ref.at[:, rows, pl.ds(HY + EY, HY)],
                STAGE + 1,
                place(sec, 0, -1),
            ),
        ]

    def advance(rate, prepare):
        prepare(odd, 2, WX - 2)

        def second(x, carry):
            for c, k in enumerate(rate(odd, x)):
                state = start[c, x] + (0.5 * STEP_DT) * k
                even[c, x, HY : HY + EY] = state[HY : HY + EY]
                slope[c, x] += 2.0 * k
            return carry

        lax.fori_loop(4, WX - 4, second, 0)
        copies = stage_copies(even)
        for copy in copies:
            copy.start()
        for copy in copies:
            copy.wait()
        prepare(even, 4, WX - 4)

        def third(x, carry):
            for c, k in enumerate(rate(even, x)):
                odd[c, x] = start[c, x] + STEP_DT * k
                slope[c, x] += 2.0 * k
            return carry

        lax.fori_loop(6, WX - 6, third, 0)
        prepare(odd, 6, WX - 6)

        def fourth(x, carry):
            for c, k in enumerate(rate(odd, x)):
                state = start[c, x] + (STEP_DT / 6.0) * (slope[c, x] + k)
                out[0, c, x - EX] = state[HY : HY + EY]
            return carry

        lax.fori_loop(EX, 2 * EX, fourth, 0)

    load_start.wait()

    @pl.when(is_flow)
    def _():
        for i in every:
            field_copy(i).wait_recv()

        def rate(ref, x):
            return flow_row(ref, flux_x, x)

        def prepare(ref, low, high):
            fluxes_x(ref, flux_x, low, high)

        prepare(start, 0, WX)

        def one(x, carry):
            for c, k in enumerate(rate(start, x)):
                odd[c, x] = start[c, x] + (0.5 * STEP_DT) * k
                slope[c, x] = k
            return carry

        lax.fori_loop(2, WX - 2, one, 0)
        advance(rate, prepare)
        partner_copy.wait_send()

    @pl.when(is_sound)
    def _():
        partner_copy.wait_recv()
        for i in level:
            speed_copy(i).start()

        @pl.when(gx < nx - 1)
        def _():
            for i in up:
                speed_copy(i).start()

        @pl.when(gx > 0)
        def _():
            for i in down:
                speed_copy(i).start()

        for i in every:
            field_copy(i).wait_recv()
            mean_copy(i).wait_recv()
        load_inner.wait()

        def plain(x, carry):
            for c, k in enumerate(sound_row(start, mean, x)):
                slope[c, x] = k
            return carry

        lax.fori_loop(2, WX - 2, plain, 0)
        for i in every:
            speed_copy(i).wait_recv()

        cells = nx * EX

        def one(x, carry):
            block = lax.rem(gx * EX + x - EX + cells, cells) // MBLEN
            mask = blocks[block].astype(jnp.float32)
            terms = [mask * part for part in lamb_row(speed, x)]
            for c in range(5):
                k = slope[c, x]
                if 1 <= c <= 3:
                    source[c - 1, x] = terms[c - 1]
                    k = k - terms[c - 1]
                    slope[c, x] = k
                odd[c, x] = start[c, x] + (0.5 * STEP_DT) * k
            return carry

        lax.fori_loop(2, WX - 2, one, 0)

        def rate(ref, x):
            rates = sound_row(ref, mean, x)
            return [
                k - source[c - 1, x] if 1 <= c <= 3 else k for c, k in enumerate(rates)
            ]

        advance(rate, lambda ref, low, high: None)
        for i in level:
            speed_copy(i).wait_send()

        @pl.when(gx < nx - 1)
        def _():
            for i in up:
                speed_copy(i).wait_send()

        @pl.when(gx > 0)
        def _():
            for i in down:
                speed_copy(i).wait_send()

        for i in every:
            mean_copy(i).wait_send()

    for i in every:
        field_copy(i).wait_send()

    @pl.when(is_flow & last)
    def _():
        for i in up:
            speed_around(i).wait_send()

    @pl.when(is_flow & first)
    def _():
        for i in down:
            speed_around(i).wait_send()


def solution(mesh):
    nx, nr = mesh.shape["gx"], mesh.shape["row"]

    def local(fields, mean_flow, source_blocks):
        window = (WX, WY, 128)
        return pl.pallas_call(
            functools.partial(kernel, nx, nr),
            out_shape=jax.ShapeDtypeStruct(fields.shape, jnp.float32),
            in_specs=[
                pl.BlockSpec(memory_space=pl.ANY),
                pl.BlockSpec(memory_space=pl.ANY),
                pl.BlockSpec(memory_space=pltpu.SMEM),
            ],
            out_specs=pl.BlockSpec(memory_space=pltpu.VMEM),
            scratch_shapes=[
                pltpu.VMEM((5, EX, EY, 128), jnp.float32),
                pltpu.VMEM((5, EX, EY, 128), jnp.float32),
                pltpu.VMEM((3, EX, EY, 128), jnp.float32),
                pltpu.VMEM((5,) + window, jnp.float32),
                pltpu.VMEM((5,) + window, jnp.float32),
                pltpu.VMEM((3,) + window, jnp.float32),
                pltpu.VMEM((3,) + window, jnp.float32),
                pltpu.VMEM((5,) + window, jnp.float32),
                pltpu.VMEM((5,) + window, jnp.float32),
                pltpu.VMEM((4,) + window, jnp.float32),
                pltpu.VMEM((5,) + window, jnp.float32),
                pltpu.SemaphoreType.DMA((SEMAPHORES,)),
                pltpu.SemaphoreType.DMA((SEMAPHORES,)),
                pltpu.SemaphoreType.DMA((4,)),
            ],
            compiler_params=pltpu.CompilerParams(collective_id=0, has_side_effects=True),
        )(fields, mean_flow, source_blocks)

    return jax.shard_map(
        local,
        mesh=mesh,
        in_specs=(P("sec", None, "gx", "row", None), P(None, "gx", "row", None), P()),
        out_specs=P("sec", None, "gx", "row", None),
        check_vma=False,
    )
```

```python
import functools

import jax
import jax.numpy as jnp
from jax import lax
from jax.experimental import pallas as pl
from jax.experimental.pallas import tpu as pltpu
from jax.sharding import PartitionSpec as P

MESH = pl.DeviceIdType.MESH
MBLEN = 4
GAMMA = 1.4
STEP_DT = 0.2
VISCOSITY = 0.05

OWN = 8
HALO = 4
WIDE = OWN + 2 * HALO

DIRECTIONS = ((1, 0), (-1, 0), (0, 1), (0, -1), (1, 1), (1, -1), (-1, 1), (-1, -1))

FIELD, SPEED, STAGE, MEAN, PARTNER = 0, 8, 16, 24, 32
SEMAPHORES = 33


def part(d, width):
    if d == 1:
        return OWN - width, HALO - width, width
    if d == -1:
        return 0, HALO + OWN, width
    return 0, HALO, OWN


def parts(direction, width):
    if direction[0] and direction[1]:
        width = 2
    (sx, tx, nx), (sy, ty, ny) = part(direction[0], width), part(direction[1], width)
    return (
        (slice(None), pl.ds(sx, nx), pl.ds(sy, ny)),
        (slice(None), pl.ds(HALO + sx, nx), pl.ds(HALO + sy, ny)),
        (slice(None), pl.ds(tx, nx), pl.ds(ty, ny)),
    )


def shift(values, axis, by):
    size = values.shape[axis]
    return pltpu.roll(values, (-by) % size, axis)


def derivative(values, axis):
    once = shift(values, axis, 1) - shift(values, axis, -1)
    return 8.0 * once - (shift(once, axis, 1) + shift(once, axis, -1))


def derivative_x(ref, c, x):
    return 8.0 * (ref[c, x + 1] - ref[c, x - 1]) - (ref[c, x + 2] - ref[c, x - 2])


def primitives(q):
    inverse = 1.0 / q[0]
    u = [q[1 + j] * inverse for j in range(3)]
    p = (GAMMA - 1.0) * (q[4] - 0.5 * (q[1] * u[0] + q[2] * u[1] + q[3] * u[2]))
    return u, p


def flux(q, u, p, d):
    parts = [q[1 + d]]
    for j in range(3):
        part = q[1 + j] * u[d]
        parts.append(part + p if j == d else part)
    parts.append((q[4] + p) * u[d])
    return parts


def fluxes_x(q_ref, f_ref, low, high):
    def row(x, carry):
        q = [q_ref[c, x] for c in range(5)]
        u, p = primitives(q)
        f = flux(q, u, p, 0)
        for c in range(1, 5):
            f_ref[c - 1, x] = f[c]
        return carry

    lax.fori_loop(low, high, row, 0)


def flow_row(q_ref, f_ref, x):
    q = [q_ref[c, x] for c in range(5)]
    u, p = primitives(q)
    along_y = flux(q, u, p, 1)
    along_z = flux(q, u, p, 2)
    rates = []
    for c in range(5):
        f, fc = (q_ref, 1) if c == 0 else (f_ref, c - 1)
        total = 8.0 * (f[fc, x - 1] - f[fc, x + 1]) + (f[fc, x + 2] - f[fc, x - 2])
        total += (16.0 * VISCOSITY) * (q_ref[c, x + 1] + q_ref[c, x - 1])
        total -= VISCOSITY * (q_ref[c, x + 2] + q_ref[c, x - 2])
        total -= (90.0 * VISCOSITY) * q[c]
        near, far = ((16.0 * VISCOSITY) * q[c], VISCOSITY * q[c])
        for axis, parts in ((0, along_y), (1, along_z)):
            eight = 8.0 * parts[c]
            total += shift(near - eight, axis, 1) + shift(near + eight, axis, -1)
            total += shift(parts[c] - far, axis, 2) - shift(parts[c] + far, axis, -2)
        rates.append(total * (1.0 / 12.0))
    return rates


def sound_row(a_ref, mean_ref, x):
    mean = [mean_ref[c, x] for c in range(5)]
    speed = [mean[j] * (1.0 / 12.0) for j in range(3)]
    density = mean[3] * (1.0 / 12.0)
    inverse = (1.0 / 12.0) / mean[3]
    slopes, carried = [], []
    for c in range(5):
        value = a_ref[c, x]
        d = [derivative_x(a_ref, c, x), derivative(value, 0), derivative(value, 1)]
        slopes.append(d)
        carried.append(speed[0] * d[0] + speed[1] * d[1] + speed[2] * d[2])
    divergence = density * (slopes[1][0] + slopes[2][1] + slopes[3][2])
    rates = [-carried[0] - divergence]
    for j in range(3):
        rates.append(-carried[1 + j] - slopes[4][j] * inverse)
    rates.append(-carried[4] - mean[4] * mean[4] * divergence)
    return rates


def lamb_row(u_ref, x):
    u = [u_ref[c, x] for c in range(3)]
    spin = (
        derivative(u[2], 0) - derivative(u[1], 1),
        derivative(u[0], 1) - derivative_x(u_ref, 2, x),
        derivative_x(u_ref, 1, x) - derivative(u[0], 0),
    )
    scale = 1.0 / 12.0
    return [
        scale * (spin[1] * u[2] - spin[2] * u[1]),
        scale * (spin[2] * u[0] - spin[0] * u[2]),
        scale * (spin[0] * u[1] - spin[1] * u[0]),
    ]


def kernel(
    nx,
    nr,
    fields,
    mean_flow,
    blocks,
    out,
    own,
    own_mean,
    own_speed,
    start,
    mean,
    speed,
    source,
    odd,
    even,
    flux_x,
    slope,
    send,
    receive,
    local,
    ready,
):
    sec = lax.axis_index("sec")
    gx = lax.axis_index("gx")
    row = lax.axis_index("row")
    is_flow = sec == 0
    is_sound = sec == 1
    first, last = gx == 0, gx == nx - 1

    def place(section, dx, dy):
        return {
            "sec": section,
            "gx": lax.rem(gx + dx + nx, nx),
            "row": lax.rem(row + dy + nr, nr),
        }

    barrier = pltpu.get_barrier_semaphore()

    def greet(device):
        pl.semaphore_signal(barrier, inc=1, device_id=device, device_id_type=MESH)

    for dx, dy in DIRECTIONS:
        greet(place(sec, dx, dy))

    @pl.when((is_sound & (gx < nx - 1)) | (is_flow & last))
    def _():
        greet(place(1 - sec, 0, 0))

    @pl.when(is_sound & first)
    def _():
        for dy in (-1, 0, 1):
            greet(place(0, -1, dy))

    @pl.when(is_sound & last)
    def _():
        for dy in (-1, 0, 1):
            greet(place(0, 1, dy))

    inner = (slice(None), pl.ds(HALO, OWN), pl.ds(HALO, OWN))
    load = pltpu.make_async_copy(fields.at[0], own, local.at[0])
    load.start()
    load_start = pltpu.make_async_copy(fields.at[0], start.at[inner], local.at[1])
    load_start.start()
    load_mean = pltpu.make_async_copy(mean_flow, own_mean, local.at[2])
    load_inner = pltpu.make_async_copy(mean_flow, mean.at[inner], local.at[3])

    @pl.when(is_sound)
    def _():
        load_mean.start()
        load_inner.start()

    load.wait()

    @pl.when(is_flow)
    def _():
        for x in range(OWN):
            inverse = 1.0 / own[0, x]
            for j in range(3):
                own_speed[j, x] = own[1 + j, x] * inverse

    @pl.when(is_sound)
    def _():
        load_mean.wait()

    for found, peers in (
        (is_flow & first, 12),
        (is_flow & (gx > 0) & (gx < nx - 1), 9),
        (is_flow & last, 11),
        (is_sound & (gx < nx - 1), 8),
        (is_sound & last, 9),
    ):

        @pl.when(found)
        def _():
            pl.semaphore_wait(barrier, peers)

    @pl.when(is_sound & last)
    def _():
        pl.semaphore_signal(ready, inc=1, device_id=place(0, 0, 0), device_id_type=MESH)

    def remote(origin, target, index, device):
        return pltpu.make_async_remote_copy(
            src_ref=origin,
            dst_ref=target,
            send_sem=send.at[index],
            recv_sem=receive.at[index],
            device_id=device,
            device_id_type=MESH,
        )

    def copies(section, origin, held, target, base, count=8, width=HALO):
        made = []
        for i in range(count):
            block, middle, slot = parts(DIRECTIONS[i], width)
            made.append(
                remote(
                    origin.at[middle if held else block],
                    target.at[slot],
                    base + i,
                    place(section, *DIRECTIONS[i]),
                )
            )
        return made

    field_copies = copies(sec, own, False, start, FIELD)
    mean_copies = copies(1, own_mean, False, mean, MEAN, count=4, width=2)
    speed_copies = copies(1, speed, True, speed, SPEED)
    around = copies(1, own_speed, False, speed, SPEED)
    stage_copies = copies(sec, even, True, even, STAGE)
    partner_copy = remote(own_speed, speed.at[inner], PARTNER, place(1, 0, 0))
    up = [i for i, d in enumerate(DIRECTIONS) if d[0] == 1]
    down = [i for i, d in enumerate(DIRECTIONS) if d[0] == -1]
    level = [i for i, d in enumerate(DIRECTIONS) if d[0] == 0]

    @pl.when(is_flow & (gx < nx - 1))
    def _():
        partner_copy.start()

    for copy in field_copies:
        copy.start()

    @pl.when(is_flow & first)
    def _():
        for i in down:
            around[i].start()

    @pl.when(is_flow & last)
    def _():
        for i in up:
            around[i].start()
        pl.semaphore_wait(ready, 1)
        partner_copy.start()

    @pl.when(is_sound)
    def _():
        for copy in mean_copies:
            copy.start()

    def advance(rate, prepare):
        prepare(odd, 2, WIDE - 2)

        def second(x, carry):
            for c, k in enumerate(rate(odd, x)):
                state = start[c, x] + (0.5 * STEP_DT) * k
                even[c, x, HALO : HALO + OWN] = state[HALO : HALO + OWN]
                slope[c, x] += 2.0 * k
            return carry

        lax.fori_loop(HALO, HALO + OWN, second, 0)
        for copy in stage_copies:
            copy.start()
        for copy in stage_copies:
            copy.wait()
        prepare(even, 0, WIDE)

        def third(x, carry):
            for c, k in enumerate(rate(even, x)):
                odd[c, x] = start[c, x] + STEP_DT * k
                slope[c, x] += 2.0 * k
            return carry

        lax.fori_loop(2, WIDE - 2, third, 0)
        prepare(odd, 2, WIDE - 2)

        def fourth(x, carry):
            for c, k in enumerate(rate(odd, x)):
                state = start[c, x] + (STEP_DT / 6.0) * (slope[c, x] + k)
                out[0, c, x - HALO] = state[HALO : HALO + OWN]
            return carry

        lax.fori_loop(HALO, HALO + OWN, fourth, 0)

    load_start.wait()

    @pl.when(is_flow)
    def _():
        for copy in field_copies:
            copy.wait_recv()

        def rate(ref, x):
            return flow_row(ref, flux_x, x)

        def prepare(ref, low, high):
            fluxes_x(ref, flux_x, low, high)

        prepare(start, 0, WIDE)

        def one(x, carry):
            for c, k in enumerate(rate(start, x)):
                odd[c, x] = start[c, x] + (0.5 * STEP_DT) * k
                slope[c, x] = k
            return carry

        lax.fori_loop(2, WIDE - 2, one, 0)

        advance(rate, prepare)
        partner_copy.wait_send()

    @pl.when(is_sound)
    def _():
        partner_copy.wait_recv()
        for i in level:
            speed_copies[i].start()

        @pl.when(gx < nx - 1)
        def _():
            for i in up:
                speed_copies[i].start()

        @pl.when(gx > 0)
        def _():
            for i in down:
                speed_copies[i].start()

        for copy in field_copies + mean_copies:
            copy.wait_recv()
        load_inner.wait()

        def plain(x, carry):
            for c, k in enumerate(sound_row(start, mean, x)):
                slope[c, x] = k
            return carry

        lax.fori_loop(2, WIDE - 2, plain, 0)
        for copy in speed_copies:
            copy.wait_recv()

        cells = nx * OWN

        def one(x, carry):
            block = lax.rem(gx * OWN + x - HALO + cells, cells) // MBLEN
            mask = blocks[block].astype(jnp.float32)
            terms = [mask * part for part in lamb_row(speed, x)]
            for c in range(5):
                k = slope[c, x]
                if 1 <= c <= 3:
                    source[c - 1, x] = terms[c - 1]
                    k = k - terms[c - 1]
                    slope[c, x] = k
                odd[c, x] = start[c, x] + (0.5 * STEP_DT) * k
            return carry

        lax.fori_loop(2, WIDE - 2, one, 0)

        def rate(ref, x):
            rates = sound_row(ref, mean, x)
            return [
                k - source[c - 1, x] if 1 <= c <= 3 else k for c, k in enumerate(rates)
            ]

        advance(rate, lambda ref, low, high: None)
        for i in level:
            speed_copies[i].wait_send()

        @pl.when(gx < nx - 1)
        def _():
            for i in up:
                speed_copies[i].wait_send()

        @pl.when(gx > 0)
        def _():
            for i in down:
                speed_copies[i].wait_send()

        for copy in mean_copies:
            copy.wait_send()

    for copy in field_copies:
        copy.wait_send()

    @pl.when(is_flow & last)
    def _():
        for i in up:
            around[i].wait_send()

    @pl.when(is_flow & first)
    def _():
        for i in down:
            around[i].wait_send()


def solution(mesh):
    nx, nr = mesh.shape["gx"], mesh.shape["row"]

    def local(fields, mean_flow, source_blocks):
        window = (WIDE, WIDE, 128)
        return pl.pallas_call(
            functools.partial(kernel, nx, nr),
            out_shape=jax.ShapeDtypeStruct(fields.shape, jnp.float32),
            in_specs=[
                pl.BlockSpec(memory_space=pl.ANY),
                pl.BlockSpec(memory_space=pl.ANY),
                pl.BlockSpec(memory_space=pltpu.SMEM),
            ],
            out_specs=pl.BlockSpec(memory_space=pltpu.VMEM),
            scratch_shapes=[
                pltpu.VMEM((5, OWN, OWN, 128), jnp.float32),
                pltpu.VMEM((5, OWN, OWN, 128), jnp.float32),
                pltpu.VMEM((3, OWN, OWN, 128), jnp.float32),
                pltpu.VMEM((5,) + window, jnp.float32),
                pltpu.VMEM((5,) + window, jnp.float32),
                pltpu.VMEM((3,) + window, jnp.float32),
                pltpu.VMEM((3,) + window, jnp.float32),
                pltpu.VMEM((5,) + window, jnp.float32),
                pltpu.VMEM((5,) + window, jnp.float32),
                pltpu.VMEM((4,) + window, jnp.float32),
                pltpu.VMEM((5,) + window, jnp.float32),
                pltpu.SemaphoreType.DMA((SEMAPHORES,)),
                pltpu.SemaphoreType.DMA((SEMAPHORES,)),
                pltpu.SemaphoreType.DMA((4,)),
                pltpu.SemaphoreType.REGULAR,
            ],
            compiler_params=pltpu.CompilerParams(collective_id=0, has_side_effects=True),
        )(fields, mean_flow, source_blocks)

    return jax.shard_map(
        local,
        mesh=mesh,
        in_specs=(P("sec", None, "gx", "row", None), P(None, "gx", "row", None), P()),
        out_specs=P("sec", None, "gx", "row", None),
        check_vma=False,
    )
```

```python
import functools

import jax
import jax.numpy as jnp
from jax import lax
from jax.experimental import pallas as pl
from jax.experimental.pallas import tpu as pltpu
from jax.sharding import PartitionSpec as P

MESH = pl.DeviceIdType.MESH
MBLEN = 4
GAMMA = 1.4
STEP_DT = 0.2
VISCOSITY = 0.05

OWN = 8
HALO = 4
BEGIN = (HALO, 8)
WINDOW = (OWN + 2 * HALO, 24, 128)

DIRECTIONS = ((1, 0), (-1, 0), (0, 1), (0, -1), (1, 1), (1, -1), (-1, 1), (-1, -1))

FIELD, SPEED, STAGE, MEAN, PARTNER = 0, 8, 16, 24, 32
SEMAPHORES = 33


def part(d, width, begin):
    if d == 1:
        return OWN - width, begin - width, width
    if d == -1:
        return 0, begin + OWN, width
    return 0, begin, OWN


def parts(direction, width):
    if direction[0] and direction[1]:
        width = 2
    both = [part(d, width, begin) for d, begin in zip(direction, BEGIN)]
    every = (slice(None),)
    return (
        every + tuple(pl.ds(s, n) for s, _, n in both),
        every + tuple(pl.ds(begin + s, n) for (s, _, n), begin in zip(both, BEGIN)),
        every + tuple(pl.ds(t, n) for _, t, n in both),
    )


def turn(values, by):
    return pltpu.roll(values, (-by) % values.shape[-1], values.ndim - 1)


class Block:
    def __init__(self, x, columns, y, rows):
        self.x, self.columns, self.y, self.rows = x, columns, y, rows

    def at(self, dx=0, dy=0):
        return (pl.ds(self.x + dx, self.columns), pl.ds(self.y + dy, self.rows))

    def get(self, ref, c, dx=0, dy=0):
        return ref[(c,) + self.at(dx, dy)]

    def put(self, ref, c, values):
        ref[(c,) + self.at()] = values


def tall(x):
    return Block(x, 1, BEGIN[1] - HALO, OWN + 2 * HALO)


def flat(x):
    return Block(x, 2, BEGIN[1], OWN)


def sweep(body, wide, count=2):
    low, high = BEGIN[0], BEGIN[0] + OWN

    def own(i, carry):
        body(flat(low + 2 * i))
        return carry

    def own_tall(x, carry):
        body(tall(x))
        return carry

    def side(i, carry):
        half = count // 2
        body(flat(jnp.where(i < half, low - count + 2 * i, high + 2 * (i - half))))
        return carry

    if wide:
        lax.fori_loop(0, count, side, 0)
        lax.fori_loop(low, high, own_tall, 0)
    else:
        lax.fori_loop(0, OWN // 2, own, 0)


def derivatives(ref, c, block, axes=(0, 1, 2)):
    found = []
    for axis in axes:
        if axis == 2:
            value = block.get(ref, c)
            once = turn(value, 1) - turn(value, -1)
            found.append(8.0 * once - (turn(once, 1) + turn(once, -1)))
        else:
            near, far = [
                block.get(ref, c, *((by, 0) if axis == 0 else (0, by)))
                - block.get(ref, c, *((-by, 0) if axis == 0 else (0, -by)))
                for by in (1, 2)
            ]
            found.append(8.0 * near - far)
    return found


def fluxes(q_ref, f_ref, block):
    q = [block.get(q_ref, c) for c in range(5)]
    inverse = 1.0 / q[0]
    u = [q[1 + j] * inverse for j in range(3)]
    p = (GAMMA - 1.0) * (q[4] - 0.5 * (q[1] * u[0] + q[2] * u[1] + q[3] * u[2]))
    h = q[4] + p
    for d in range(3):
        for j in range(3):
            part = q[1 + j] * u[d]
            block.put(f_ref, 4 * d + j, part + p if j == d else part)
        block.put(f_ref, 4 * d + 3, h * u[d])


def flow_rates(q_ref, f_ref, block):
    rates = []
    for c in range(5):
        f = [(q_ref, 1 + d) if c == 0 else (f_ref, 4 * d + c - 1) for d in range(3)]
        sums = []
        for by in (1, 2):
            ahead, behind = ((by, 0), (0, by)), ((-by, 0), (0, -by))
            flow = [
                block.get(*f[d], *behind[d]) - block.get(*f[d], *ahead[d]) for d in range(2)
            ]
            spread = [
                block.get(q_ref, c, *ahead[d]) + block.get(q_ref, c, *behind[d]) for d in range(2)
            ]
            sums.append((flow[0] + flow[1], spread[0] + spread[1]))
        q, along = block.get(q_ref, c), block.get(*f[2])
        eight, near, far = 8.0 * along, (16.0 * VISCOSITY) * q, VISCOSITY * q
        total = 8.0 * sums[0][0] - sums[1][0] + (16.0 * VISCOSITY) * sums[0][1]
        total -= VISCOSITY * sums[1][1] + (90.0 * VISCOSITY) * q
        total += turn(near - eight, 1) + turn(near + eight, -1)
        total += turn(along - far, 2) - turn(along + far, -2)
        rates.append(total * (1.0 / 12.0))
    return rates


def sound_rates(a_ref, mean_ref, block):
    mean = [block.get(mean_ref, c) for c in range(5)]
    speed = [mean[j] * (1.0 / 12.0) for j in range(3)]
    density = mean[3] * (1.0 / 12.0)
    inverse = (1.0 / 12.0) / mean[3]
    slopes = [derivatives(a_ref, c, block) for c in range(5)]
    carried = [speed[0] * d[0] + speed[1] * d[1] + speed[2] * d[2] for d in slopes]
    divergence = density * (slopes[1][0] + slopes[2][1] + slopes[3][2])
    rates = [-carried[0] - divergence]
    for j in range(3):
        rates.append(-carried[1 + j] - slopes[4][j] * inverse)
    rates.append(-carried[4] - mean[4] * mean[4] * divergence)
    return rates


def lamb(u_ref, block):
    u = [block.get(u_ref, c) * (1.0 / 12.0) for c in range(3)]
    d = [derivatives(u_ref, c, block, tuple(k for k in range(3) if k != c)) for c in range(3)]
    spin = (d[2][1] - d[1][1], d[0][1] - d[2][0], d[1][0] - d[0][0])
    return [
        spin[1] * u[2] - spin[2] * u[1],
        spin[2] * u[0] - spin[0] * u[2],
        spin[0] * u[1] - spin[1] * u[0],
    ]


def kernel(
    nx,
    nr,
    fields,
    mean_flow,
    blocks,
    out,
    own,
    own_mean,
    own_speed,
    start,
    mean,
    speed,
    source,
    odd,
    even,
    flux,
    slope,
    send,
    receive,
    local,
    ready,
):
    sec = lax.axis_index("sec")
    gx = lax.axis_index("gx")
    row = lax.axis_index("row")
    is_flow = sec == 0
    is_sound = sec == 1
    first, last = gx == 0, gx == nx - 1

    def place(section, dx, dy):
        return {
            "sec": section,
            "gx": lax.rem(gx + dx + nx, nx),
            "row": lax.rem(row + dy + nr, nr),
        }

    barrier = pltpu.get_barrier_semaphore()

    def greet(device):
        pl.semaphore_signal(barrier, inc=1, device_id=device, device_id_type=MESH)

    for dx, dy in DIRECTIONS:
        greet(place(sec, dx, dy))

    @pl.when((is_sound & (gx < nx - 1)) | (is_flow & last))
    def _():
        greet(place(1 - sec, 0, 0))

    @pl.when(is_sound & first)
    def _():
        for dy in (-1, 0, 1):
            greet(place(0, -1, dy))

    @pl.when(is_sound & last)
    def _():
        for dy in (-1, 0, 1):
            greet(place(0, 1, dy))

    inner = (slice(None), pl.ds(BEGIN[0], OWN), pl.ds(BEGIN[1], OWN))
    load = pltpu.make_async_copy(fields.at[0], own, local.at[0])
    load.start()
    load_start = pltpu.make_async_copy(fields.at[0], start.at[inner], local.at[1])
    load_start.start()
    load_mean = pltpu.make_async_copy(mean_flow, own_mean, local.at[2])
    load_inner = pltpu.make_async_copy(mean_flow, mean.at[inner], local.at[3])

    @pl.when(is_sound)
    def _():
        load_mean.start()
        load_inner.start()

    load.wait()

    @pl.when(is_flow)
    def _():
        for x in range(OWN):
            inverse = 1.0 / own[0, x]
            for j in range(3):
                own_speed[j, x] = own[1 + j, x] * inverse

    @pl.when(is_sound)
    def _():
        load_mean.wait()

    for found, peers in (
        (is_flow & first, 12),
        (is_flow & (gx > 0) & (gx < nx - 1), 9),
        (is_flow & last, 11),
        (is_sound & (gx < nx - 1), 8),
        (is_sound & last, 9),
    ):

        @pl.when(found)
        def _():
            pl.semaphore_wait(barrier, peers)

    @pl.when(is_sound & last)
    def _():
        pl.semaphore_signal(ready, inc=1, device_id=place(0, 0, 0), device_id_type=MESH)

    def remote(origin, target, index, device):
        return pltpu.make_async_remote_copy(
            src_ref=origin,
            dst_ref=target,
            send_sem=send.at[index],
            recv_sem=receive.at[index],
            device_id=device,
            device_id_type=MESH,
        )

    def copies(section, origin, held, target, base, count=8, width=HALO):
        made = []
        for i in range(count):
            block, middle, slot = parts(DIRECTIONS[i], width)
            made.append(
                remote(
                    origin.at[middle if held else block],
                    target.at[slot],
                    base + i,
                    place(section, *DIRECTIONS[i]),
                )
            )
        return made

    field_copies = copies(sec, own, False, start, FIELD)
    mean_copies = copies(1, own_mean, False, mean, MEAN, count=4, width=2)
    speed_copies = copies(1, speed, True, speed, SPEED)
    around = copies(1, own_speed, False, speed, SPEED)
    stage_copies = copies(sec, even, True, even, STAGE)
    partner_copy = remote(own_speed, speed.at[inner], PARTNER, place(1, 0, 0))
    up = [i for i, d in enumerate(DIRECTIONS) if d[0] == 1]
    down = [i for i, d in enumerate(DIRECTIONS) if d[0] == -1]
    level = [i for i, d in enumerate(DIRECTIONS) if d[0] == 0]

    for copy in field_copies:
        copy.start()

    @pl.when(is_flow & (gx < nx - 1))
    def _():
        partner_copy.start()

    @pl.when(is_flow & first)
    def _():
        for i in down:
            around[i].start()

    @pl.when(is_flow & last)
    def _():
        for i in up:
            around[i].start()
        pl.semaphore_wait(ready, 1)
        partner_copy.start()

    @pl.when(is_sound)
    def _():
        for copy in mean_copies:
            copy.start()

    def advance(rate, prepare):
        prepare(odd, False)

        def second(block):
            for c, k in enumerate(rate(odd, block)):
                block.put(even, c, block.get(start, c) + (0.5 * STEP_DT) * k)
                block.put(slope, c, block.get(slope, c) + 2.0 * k)

        sweep(second, False)
        for copy in stage_copies:
            copy.start()
        for copy in stage_copies:
            copy.wait()
        prepare(even, True)

        def third(block):
            for c, k in enumerate(rate(even, block)):
                block.put(odd, c, block.get(start, c) + STEP_DT * k)
                block.put(slope, c, block.get(slope, c) + 2.0 * k)

        sweep(third, True)
        prepare(odd, False)

        def fourth(block):
            for c, k in enumerate(rate(odd, block)):
                state = block.get(start, c) + (STEP_DT / 6.0) * (block.get(slope, c) + k)
                out[0, c, pl.ds(block.x - BEGIN[0], block.columns)] = state

        sweep(fourth, False)

    load_start.wait()

    @pl.when(is_flow)
    def _():
        for copy in field_copies:
            copy.wait_recv()

        def rate(ref, block):
            return flow_rates(ref, flux, block)

        def prepare(ref, wide):
            low, high = BEGIN[0], BEGIN[0] + OWN
            reach = HALO if wide else 2

            def columns(i, carry):
                fluxes(ref, flux, tall(low - reach + 2 + i))
                return carry

            def ends(i, carry):
                fluxes(ref, flux, flat(jnp.where(i == 0, low - reach, high + reach - 2)))
                return carry

            lax.fori_loop(0, 2, ends, 0)
            lax.fori_loop(0, OWN + 2 * reach - 4, columns, 0)

        prepare(start, True)

        def one(block):
            for c, k in enumerate(rate(start, block)):
                block.put(odd, c, block.get(start, c) + (0.5 * STEP_DT) * k)
                block.put(slope, c, k)

        sweep(one, True)
        advance(rate, prepare)
        partner_copy.wait_send()

    @pl.when(is_sound)
    def _():
        partner_copy.wait_recv()
        for i in level:
            speed_copies[i].start()

        @pl.when(gx < nx - 1)
        def _():
            for i in up:
                speed_copies[i].start()

        @pl.when(gx > 0)
        def _():
            for i in down:
                speed_copies[i].start()

        for copy in field_copies + mean_copies:
            copy.wait_recv()
        load_inner.wait()

        def plain(block):
            for c, k in enumerate(sound_rates(start, mean, block)):
                block.put(slope, c, k)

        sweep(plain, True)
        for copy in speed_copies:
            copy.wait_recv()

        cells = nx * OWN

        def one(block):
            masks = []
            for i in range(block.columns):
                cell = lax.rem(gx * OWN + block.x + i - BEGIN[0] + cells, cells)
                masks.append(blocks[cell // MBLEN].astype(jnp.float32))
            terms = lamb(speed, block)
            for j in range(3):
                for i in range(block.columns):
                    column = Block(block.x + i, 1, block.y, block.rows)
                    column.put(source, j, masks[i] * terms[j][i : i + 1])
            for c in range(5):
                k = block.get(slope, c)
                if 1 <= c <= 3:
                    k = k - block.get(source, c - 1)
                    block.put(slope, c, k)
                block.put(odd, c, block.get(start, c) + (0.5 * STEP_DT) * k)

        sweep(one, True)

        def rate(ref, block):
            rates = sound_rates(ref, mean, block)
            return [
                k - block.get(source, c - 1) if 1 <= c <= 3 else k for c, k in enumerate(rates)
            ]

        advance(rate, lambda ref, wide: None)
        for i in level:
            speed_copies[i].wait_send()

        @pl.when(gx < nx - 1)
        def _():
            for i in up:
                speed_copies[i].wait_send()

        @pl.when(gx > 0)
        def _():
            for i in down:
                speed_copies[i].wait_send()

        for copy in mean_copies:
            copy.wait_send()

    for copy in field_copies:
        copy.wait_send()

    @pl.when(is_flow & last)
    def _():
        for i in up:
            around[i].wait_send()

    @pl.when(is_flow & first)
    def _():
        for i in down:
            around[i].wait_send()


def solution(mesh):
    nx, nr = mesh.shape["gx"], mesh.shape["row"]

    def local(fields, mean_flow, source_blocks):
        return pl.pallas_call(
            functools.partial(kernel, nx, nr),
            out_shape=jax.ShapeDtypeStruct(fields.shape, jnp.float32),
            in_specs=[
                pl.BlockSpec(memory_space=pl.ANY),
                pl.BlockSpec(memory_space=pl.ANY),
                pl.BlockSpec(memory_space=pltpu.SMEM),
            ],
            out_specs=pl.BlockSpec(memory_space=pltpu.VMEM),
            scratch_shapes=[
                pltpu.VMEM((5, OWN, OWN, 128), jnp.float32),
                pltpu.VMEM((5, OWN, OWN, 128), jnp.float32),
                pltpu.VMEM((3, OWN, OWN, 128), jnp.float32),
                pltpu.VMEM((5,) + WINDOW, jnp.float32),
                pltpu.VMEM((5,) + WINDOW, jnp.float32),
                pltpu.VMEM((3,) + WINDOW, jnp.float32),
                pltpu.VMEM((3,) + WINDOW, jnp.float32),
                pltpu.VMEM((5,) + WINDOW, jnp.float32),
                pltpu.VMEM((5,) + WINDOW, jnp.float32),
                pltpu.VMEM((12,) + WINDOW, jnp.float32),
                pltpu.VMEM((5,) + WINDOW, jnp.float32),
                pltpu.SemaphoreType.DMA((SEMAPHORES,)),
                pltpu.SemaphoreType.DMA((SEMAPHORES,)),
                pltpu.SemaphoreType.DMA((4,)),
                pltpu.SemaphoreType.REGULAR,
            ],
            compiler_params=pltpu.CompilerParams(collective_id=0, has_side_effects=True),
        )(fields, mean_flow, source_blocks)

    return jax.shard_map(
        local,
        mesh=mesh,
        in_specs=(P("sec", None, "gx", "row", None), P(None, "gx", "row", None), P()),
        out_specs=P("sec", None, "gx", "row", None),
        check_vma=False,
    )
```

```python
import functools

import jax
import jax.numpy as jnp
from jax import lax
from jax.experimental import pallas as pl
from jax.experimental.pallas import tpu as pltpu
from jax.sharding import PartitionSpec as P

MESH = pl.DeviceIdType.MESH
MBLEN = 4
GAMMA = 1.4
STEP_DT = 0.2
VISCOSITY = 0.05

OWN = 8
HALO = 4
BEGIN = (HALO, 8)
WINDOW = (OWN + 2 * HALO, 24, 128)

DIRECTIONS = ((1, 0), (-1, 0), (0, 1), (0, -1), (1, 1), (1, -1), (-1, 1), (-1, -1))

FIELD, SPEED, STAGE, MEAN, PARTNER = 0, 8, 16, 24, 32
SEMAPHORES = 33


def part(d, width, begin):
    if d == 1:
        return OWN - width, begin - width, width
    if d == -1:
        return 0, begin + OWN, width
    return 0, begin, OWN


def parts(direction, width):
    if direction[0] and direction[1]:
        width = 2
    both = [part(d, width, begin) for d, begin in zip(direction, BEGIN)]
    every = (slice(None),)
    return (
        every + tuple(pl.ds(s, n) for s, _, n in both),
        every + tuple(pl.ds(begin + s, n) for (s, _, n), begin in zip(both, BEGIN)),
        every + tuple(pl.ds(t, n) for _, t, n in both),
    )


def turn(values, by):
    return pltpu.roll(values, (-by) % values.shape[-1], values.ndim - 1)


class Block:
    def __init__(self, x, columns, y, rows):
        self.x, self.columns, self.y, self.rows = x, columns, y, rows

    def at(self, dx=0, dy=0):
        return (pl.ds(self.x + dx, self.columns), pl.ds(self.y + dy, self.rows))

    def get(self, ref, c, dx=0, dy=0):
        return ref[(c,) + self.at(dx, dy)]

    def put(self, ref, c, values):
        ref[(c,) + self.at()] = values


def tall(x):
    return Block(x, 1, BEGIN[1] - HALO, OWN + 2 * HALO)


def flat(x):
    return Block(x, 2, BEGIN[1], OWN)


def sweep(body, wide, count=2):
    low, high = BEGIN[0], BEGIN[0] + OWN

    def own(i, carry):
        body(flat(low + 2 * i))
        return carry

    def own_tall(x, carry):
        body(tall(x))
        return carry

    def side(i, carry):
        half = count // 2
        body(flat(jnp.where(i < half, low - count + 2 * i, high + 2 * (i - half))))
        return carry

    if wide:
        lax.fori_loop(0, count, side, 0)
        lax.fori_loop(low, high, own_tall, 0)
    else:
        lax.fori_loop(0, OWN // 2, own, 0)


def derivatives(ref, c, block, axes=(0, 1, 2)):
    found = []
    for axis in axes:
        if axis == 2:
            value = block.get(ref, c)
            once = turn(value, 1) - turn(value, -1)
            found.append(8.0 * once - (turn(once, 1) + turn(once, -1)))
        else:
            near, far = [
                block.get(ref, c, *((by, 0) if axis == 0 else (0, by)))
                - block.get(ref, c, *((-by, 0) if axis == 0 else (0, -by)))
                for by in (1, 2)
            ]
            found.append(8.0 * near - far)
    return found


def fluxes(q_ref, f_ref, block):
    q = [block.get(q_ref, c) for c in range(5)]
    inverse = 1.0 / q[0]
    u = [q[1 + j] * inverse for j in range(3)]
    p = (GAMMA - 1.0) * (q[4] - 0.5 * (q[1] * u[0] + q[2] * u[1] + q[3] * u[2]))
    h = q[4] + p
    for d in range(3):
        for j in range(3):
            part = q[1 + j] * u[d]
            block.put(f_ref, 4 * d + j, part + p if j == d else part)
        block.put(f_ref, 4 * d + 3, h * u[d])


def flow_rates(q_ref, f_ref, block):
    rates = []
    for c in range(5):
        f = [(q_ref, 1 + d) if c == 0 else (f_ref, 4 * d + c - 1) for d in range(3)]
        sums = []
        for by in (1, 2):
            ahead, behind = ((by, 0), (0, by)), ((-by, 0), (0, -by))
            flow = [
                block.get(*f[d], *behind[d]) - block.get(*f[d], *ahead[d]) for d in range(2)
            ]
            spread = [
                block.get(q_ref, c, *ahead[d]) + block.get(q_ref, c, *behind[d]) for d in range(2)
            ]
            sums.append((flow[0] + flow[1], spread[0] + spread[1]))
        q, along = block.get(q_ref, c), block.get(*f[2])
        eight, near, far = 8.0 * along, (16.0 * VISCOSITY) * q, VISCOSITY * q
        total = 8.0 * sums[0][0] - sums[1][0] + (16.0 * VISCOSITY) * sums[0][1]
        total -= VISCOSITY * sums[1][1] + (90.0 * VISCOSITY) * q
        total += turn(near - eight, 1) + turn(near + eight, -1)
        total += turn(along - far, 2) - turn(along + far, -2)
        rates.append(total * (1.0 / 12.0))
    return rates


def sound_rates(a_ref, mean_ref, block):
    mean = [block.get(mean_ref, c) for c in range(5)]
    speed = [mean[j] * (1.0 / 12.0) for j in range(3)]
    density = mean[3] * (1.0 / 12.0)
    inverse = (1.0 / 12.0) / mean[3]
    slopes = [derivatives(a_ref, c, block) for c in range(5)]
    carried = [speed[0] * d[0] + speed[1] * d[1] + speed[2] * d[2] for d in slopes]
    divergence = density * (slopes[1][0] + slopes[2][1] + slopes[3][2])
    rates = [-carried[0] - divergence]
    for j in range(3):
        rates.append(-carried[1 + j] - slopes[4][j] * inverse)
    rates.append(-carried[4] - mean[4] * mean[4] * divergence)
    return rates


def lamb(u_ref, block):
    u = [block.get(u_ref, c) * (1.0 / 12.0) for c in range(3)]
    d = [derivatives(u_ref, c, block, tuple(k for k in range(3) if k != c)) for c in range(3)]
    spin = (d[2][1] - d[1][1], d[0][1] - d[2][0], d[1][0] - d[0][0])
    return [
        spin[1] * u[2] - spin[2] * u[1],
        spin[2] * u[0] - spin[0] * u[2],
        spin[0] * u[1] - spin[1] * u[0],
    ]


def kernel(
    nx,
    nr,
    fields,
    mean_flow,
    all_blocks,
    out,
    last_slope,
    own,
    own_mean,
    own_speed,
    start,
    mean,
    speed,
    source,
    odd,
    even,
    flux,
    slope,
    send,
    receive,
    local,
    ready,
    blocks,
):
    sec = lax.axis_index("sec")
    gx = lax.axis_index("gx")
    row = lax.axis_index("row")
    is_flow = sec == 0
    is_sound = sec == 1
    first, last = gx == 0, gx == nx - 1

    def place(section, dx, dy):
        return {
            "sec": section,
            "gx": lax.rem(gx + dx + nx, nx),
            "row": lax.rem(row + dy + nr, nr),
        }

    barrier = pltpu.get_barrier_semaphore()

    def greet(device):
        pl.semaphore_signal(barrier, inc=1, device_id=device, device_id_type=MESH)

    for dx, dy in DIRECTIONS:
        greet(place(sec, dx, dy))

    @pl.when((is_sound & (gx < nx - 1)) | (is_flow & last))
    def _():
        greet(place(1 - sec, 0, 0))

    @pl.when(is_sound & first)
    def _():
        for dy in (-1, 0, 1):
            greet(place(0, -1, dy))

    @pl.when(is_sound & last)
    def _():
        for dy in (-1, 0, 1):
            greet(place(0, 1, dy))

    inner = (slice(None), pl.ds(BEGIN[0], OWN), pl.ds(BEGIN[1], OWN))
    load = pltpu.make_async_copy(fields.at[0], own, local.at[0])
    load.start()
    load_start = pltpu.make_async_copy(fields.at[0], start.at[inner], local.at[1])
    load_start.start()
    load_mean = pltpu.make_async_copy(mean_flow, own_mean, local.at[2])
    load_blocks = pltpu.make_async_copy(all_blocks, blocks, local.at[4])
    load_inner = pltpu.make_async_copy(mean_flow, mean.at[inner], local.at[3])

    @pl.when(is_sound)
    def _():
        load_mean.start()
        load_inner.start()
        load_blocks.start()

    load.wait()

    @pl.when(is_flow)
    def _():
        for x in range(OWN):
            inverse = 1.0 / own[0, x]
            for j in range(3):
                own_speed[j, x] = own[1 + j, x] * inverse

    @pl.when(is_sound)
    def _():
        load_mean.wait()

    for found, peers in (
        (is_flow & first, 12),
        (is_flow & (gx > 0) & (gx < nx - 1), 9),
        (is_flow & last, 11),
        (is_sound & (gx < nx - 1), 8),
        (is_sound & last, 9),
    ):

        @pl.when(found)
        def _():
            pl.semaphore_wait(barrier, peers)

    @pl.when(is_sound & last)
    def _():
        pl.semaphore_signal(ready, inc=1, device_id=place(0, 0, 0), device_id_type=MESH)

    def remote(origin, target, index, device):
        return pltpu.make_async_remote_copy(
            src_ref=origin,
            dst_ref=target,
            send_sem=send.at[index],
            recv_sem=receive.at[index],
            device_id=device,
            device_id_type=MESH,
        )

    def copies(section, origin, held, target, base, count=8, width=HALO):
        made = []
        for i in range(count):
            block, middle, slot = parts(DIRECTIONS[i], width)
            made.append(
                remote(
                    origin.at[middle if held else block],
                    target.at[slot],
                    base + i,
                    place(section, *DIRECTIONS[i]),
                )
            )
        return made

    field_copies = copies(sec, own, False, start, FIELD)
    mean_copies = copies(1, own_mean, False, mean, MEAN, count=4, width=2)
    speed_copies = copies(1, speed, True, speed, SPEED)
    around = copies(1, own_speed, False, speed, SPEED)
    stage_copies = copies(sec, even, True, even, STAGE)
    partner_copy = remote(own_speed, speed.at[inner], PARTNER, place(1, 0, 0))
    up = [i for i, d in enumerate(DIRECTIONS) if d[0] == 1]
    down = [i for i, d in enumerate(DIRECTIONS) if d[0] == -1]
    level = [i for i, d in enumerate(DIRECTIONS) if d[0] == 0]

    for copy in field_copies:
        copy.start()

    @pl.when(is_flow & (gx < nx - 1))
    def _():
        partner_copy.start()

    @pl.when(is_flow & first)
    def _():
        for i in down:
            around[i].start()

    @pl.when(is_flow & last)
    def _():
        for i in up:
            around[i].start()
        pl.semaphore_wait(ready, 1)
        partner_copy.start()

    @pl.when(is_sound)
    def _():
        for copy in mean_copies:
            copy.start()

    def advance(rate, prepare):
        prepare(odd, False)

        def second(block):
            for c, k in enumerate(rate(odd, block)):
                block.put(even, c, block.get(start, c) + (0.5 * STEP_DT) * k)
                block.put(slope, c, block.get(slope, c) + 2.0 * k)

        sweep(second, False)
        for copy in stage_copies:
            copy.start()
        for copy in stage_copies:
            copy.wait()
        prepare(even, True)

        def third(block):
            for c, k in enumerate(rate(even, block)):
                block.put(odd, c, block.get(start, c) + STEP_DT * k)
                block.put(slope, c, block.get(slope, c) + 2.0 * k)

        sweep(third, True)
        prepare(odd, False)

        def fourth(block):
            for c, k in enumerate(rate(odd, block)):
                columns = pl.ds(block.x - BEGIN[0], block.columns)
                out[0, c, columns] = block.get(start, c) + (STEP_DT / 6.0) * block.get(slope, c)
                last_slope[0, c, columns] = k

        sweep(fourth, False)

    load_start.wait()

    @pl.when(is_flow)
    def _():
        for copy in field_copies:
            copy.wait_recv()

        def rate(ref, block):
            return flow_rates(ref, flux, block)

        def prepare(ref, wide):
            low, high = BEGIN[0], BEGIN[0] + OWN
            reach = HALO if wide else 2

            def columns(i, carry):
                fluxes(ref, flux, tall(low - reach + 2 + i))
                return carry

            def ends(i, carry):
                fluxes(ref, flux, flat(jnp.where(i == 0, low - reach, high + reach - 2)))
                return carry

            lax.fori_loop(0, 2, ends, 0)
            lax.fori_loop(0, OWN + 2 * reach - 4, columns, 0)

        prepare(start, True)

        def one(block):
            for c, k in enumerate(rate(start, block)):
                block.put(odd, c, block.get(start, c) + (0.5 * STEP_DT) * k)
                block.put(slope, c, k)

        sweep(one, True)
        advance(rate, prepare)
        partner_copy.wait_send()

    @pl.when(is_sound)
    def _():
        partner_copy.wait_recv()
        for i in level:
            speed_copies[i].start()

        @pl.when(gx < nx - 1)
        def _():
            for i in up:
                speed_copies[i].start()

        @pl.when(gx > 0)
        def _():
            for i in down:
                speed_copies[i].start()

        for copy in field_copies + mean_copies:
            copy.wait_recv()
        load_inner.wait()
        load_blocks.wait()

        def plain(block):
            for c, k in enumerate(sound_rates(start, mean, block)):
                block.put(slope, c, k)

        sweep(plain, True)
        for copy in speed_copies:
            copy.wait_recv()

        cells = nx * OWN

        def one(block):
            masks = []
            for i in range(block.columns):
                cell = lax.rem(gx * OWN + block.x + i - BEGIN[0] + cells, cells)
                masks.append(blocks[cell // MBLEN].astype(jnp.float32))
            terms = lamb(speed, block)
            for j in range(3):
                for i in range(block.columns):
                    column = Block(block.x + i, 1, block.y, block.rows)
                    column.put(source, j, masks[i] * terms[j][i : i + 1])
            for c in range(5):
                k = block.get(slope, c)
                if 1 <= c <= 3:
                    k = k - block.get(source, c - 1)
                    block.put(slope, c, k)
                block.put(odd, c, block.get(start, c) + (0.5 * STEP_DT) * k)

        sweep(one, True)

        def rate(ref, block):
            rates = sound_rates(ref, mean, block)
            return [
                k - block.get(source, c - 1) if 1 <= c <= 3 else k for c, k in enumerate(rates)
            ]

        advance(rate, lambda ref, wide: None)
        for i in level:
            speed_copies[i].wait_send()

        @pl.when(gx < nx - 1)
        def _():
            for i in up:
                speed_copies[i].wait_send()

        @pl.when(gx > 0)
        def _():
            for i in down:
                speed_copies[i].wait_send()

        for copy in mean_copies:
            copy.wait_send()

    for copy in field_copies:
        copy.wait_send()

    @pl.when(is_flow & last)
    def _():
        for i in up:
            around[i].wait_send()

    @pl.when(is_flow & first)
    def _():
        for i in down:
            around[i].wait_send()


def solution(mesh):
    nx, nr = mesh.shape["gx"], mesh.shape["row"]

    def local(fields, mean_flow, source_blocks):
        fields = pltpu.with_memory_space_constraint(fields, pltpu.HBM)
        mean_flow = pltpu.with_memory_space_constraint(mean_flow, pltpu.HBM)
        source_blocks = pltpu.with_memory_space_constraint(source_blocks, pltpu.HBM)
        state, last_slope = pl.pallas_call(
            functools.partial(kernel, nx, nr),
            out_shape=[jax.ShapeDtypeStruct(fields.shape, jnp.float32)] * 2,
            in_specs=[
                pl.BlockSpec(memory_space=pltpu.HBM),
                pl.BlockSpec(memory_space=pltpu.HBM),
                pl.BlockSpec(memory_space=pltpu.HBM),
            ],
            out_specs=[pl.BlockSpec(memory_space=pltpu.VMEM)] * 2,
            scratch_shapes=[
                pltpu.VMEM((5, OWN, OWN, 128), jnp.float32),
                pltpu.VMEM((5, OWN, OWN, 128), jnp.float32),
                pltpu.VMEM((3, OWN, OWN, 128), jnp.float32),
                pltpu.VMEM((5,) + WINDOW, jnp.float32),
                pltpu.VMEM((5,) + WINDOW, jnp.float32),
                pltpu.VMEM((3,) + WINDOW, jnp.float32),
                pltpu.VMEM((3,) + WINDOW, jnp.float32),
                pltpu.VMEM((5,) + WINDOW, jnp.float32),
                pltpu.VMEM((5,) + WINDOW, jnp.float32),
                pltpu.VMEM((12,) + WINDOW, jnp.float32),
                pltpu.VMEM((5,) + WINDOW, jnp.float32),
                pltpu.SemaphoreType.DMA((SEMAPHORES,)),
                pltpu.SemaphoreType.DMA((SEMAPHORES,)),
                pltpu.SemaphoreType.DMA((5,)),
                pltpu.SemaphoreType.REGULAR,
                pltpu.SMEM(source_blocks.shape, jnp.int32),
            ],
            compiler_params=pltpu.CompilerParams(
                collective_id=0, has_side_effects=True, vmem_limit_bytes=16 * 1024 * 1024
            ),
        )(fields, mean_flow, source_blocks)
        return state + (STEP_DT / 6.0) * last_slope

    return jax.shard_map(
        local,
        mesh=mesh,
        in_specs=(P("sec", None, "gx", "row", None), P(None, "gx", "row", None), P()),
        out_specs=P("sec", None, "gx", "row", None),
        check_vma=False,
    )
```

```python
import functools

import jax
import jax.numpy as jnp
from jax import lax
from jax.experimental import pallas as pl
from jax.experimental.pallas import tpu as pltpu
from jax.sharding import PartitionSpec as P

MESH = pl.DeviceIdType.MESH
MBLEN = 4
GAMMA = 1.4
STEP_DT = 0.2
VISCOSITY = 0.05

OWN = 8
HALO = 4
BEGIN = (HALO, 8)
WINDOW = (OWN + 2 * HALO, 24, 128)

DIRECTIONS = ((1, 0), (-1, 0), (0, 1), (0, -1), (1, 1), (1, -1), (-1, 1), (-1, -1))

FIELD, SPEED, STAGE, MEAN, PARTNER = 0, 8, 16, 24, 32
SEMAPHORES = 33


def part(d, width, begin):
    if d == 1:
        return OWN - width, begin - width, width
    if d == -1:
        return 0, begin + OWN, width
    return 0, begin, OWN


def parts(direction, width):
    if direction[0] and direction[1]:
        width = 2
    both = [part(d, width, begin) for d, begin in zip(direction, BEGIN)]
    every = (slice(None),)
    return (
        every + tuple(pl.ds(s, n) for s, _, n in both),
        every + tuple(pl.ds(begin + s, n) for (s, _, n), begin in zip(both, BEGIN)),
        every + tuple(pl.ds(t, n) for _, t, n in both),
    )


def turn(values, by):
    return pltpu.roll(values, (-by) % values.shape[-1], values.ndim - 1)


class Block:
    def __init__(self, x, columns, y, rows):
        self.x, self.columns, self.y, self.rows = x, columns, y, rows

    def at(self, dx=0, dy=0):
        return (pl.ds(self.x + dx, self.columns), pl.ds(self.y + dy, self.rows))

    def get(self, ref, c, dx=0, dy=0):
        return ref[(c,) + self.at(dx, dy)]

    def put(self, ref, c, values):
        ref[(c,) + self.at()] = values


def tall(x):
    return Block(x, 1, BEGIN[1] - HALO, OWN + 2 * HALO)


def flat(x):
    return Block(x, 2, BEGIN[1], OWN)


LOW, HIGH = BEGIN[0], BEGIN[0] + OWN


def sweep(body):
    def own(i, carry):
        body(flat(LOW + 2 * i))
        return carry

    lax.fori_loop(0, OWN // 2, own, 0)


def sweep_middle(body):
    def middle(x, carry):
        body(tall(x))
        return carry

    lax.fori_loop(LOW + 2, HIGH - 2, middle, 0)


def sweep_rest(body):
    def edge(i, carry):
        body(tall(jnp.where(i < 2, LOW + i, HIGH - 4 + i)))
        return carry

    def side(i, carry):
        body(flat(jnp.where(i == 0, LOW - 2, HIGH)))
        return carry

    lax.fori_loop(0, 4, edge, 0)
    lax.fori_loop(0, 2, side, 0)


def derivatives(ref, c, block, axes=(0, 1, 2)):
    found = []
    for axis in axes:
        if axis == 2:
            value = block.get(ref, c)
            once = turn(value, 1) - turn(value, -1)
            found.append(8.0 * once - (turn(once, 1) + turn(once, -1)))
        else:
            near, far = [
                block.get(ref, c, *((by, 0) if axis == 0 else (0, by)))
                - block.get(ref, c, *((-by, 0) if axis == 0 else (0, -by)))
                for by in (1, 2)
            ]
            found.append(8.0 * near - far)
    return found


def fluxes(q_ref, f_ref, block):
    q = [block.get(q_ref, c) for c in range(5)]
    inverse = 1.0 / q[0]
    u = [q[1 + j] * inverse for j in range(3)]
    p = (GAMMA - 1.0) * (q[4] - 0.5 * (q[1] * u[0] + q[2] * u[1] + q[3] * u[2]))
    h = q[4] + p
    for d in range(3):
        for j in range(3):
            part = q[1 + j] * u[d]
            block.put(f_ref, 4 * d + j, part + p if j == d else part)
        block.put(f_ref, 4 * d + 3, h * u[d])


def flow_rates(q_ref, f_ref, block):
    rates = []
    for c in range(5):
        f = [(q_ref, 1 + d) if c == 0 else (f_ref, 4 * d + c - 1) for d in range(3)]
        sums = []
        for by in (1, 2):
            ahead, behind = ((by, 0), (0, by)), ((-by, 0), (0, -by))
            flow = [
                block.get(*f[d], *behind[d]) - block.get(*f[d], *ahead[d]) for d in range(2)
            ]
            spread = [
                block.get(q_ref, c, *ahead[d]) + block.get(q_ref, c, *behind[d]) for d in range(2)
            ]
            sums.append((flow[0] + flow[1], spread[0] + spread[1]))
        q, along = block.get(q_ref, c), block.get(*f[2])
        eight, near, far = 8.0 * along, (16.0 * VISCOSITY) * q, VISCOSITY * q
        total = 8.0 * sums[0][0] - sums[1][0] + (16.0 * VISCOSITY) * sums[0][1]
        total -= VISCOSITY * sums[1][1] + (90.0 * VISCOSITY) * q
        total += turn(near - eight, 1) + turn(near + eight, -1)
        total += turn(along - far, 2) - turn(along + far, -2)
        rates.append(total * (1.0 / 12.0))
    return rates


def sound_rates(a_ref, mean_ref, block):
    mean = [block.get(mean_ref, c) for c in range(5)]
    speed = [mean[j] * (1.0 / 12.0) for j in range(3)]
    density = mean[3] * (1.0 / 12.0)
    inverse = (1.0 / 12.0) / mean[3]
    slopes = [derivatives(a_ref, c, block) for c in range(5)]
    carried = [speed[0] * d[0] + speed[1] * d[1] + speed[2] * d[2] for d in slopes]
    divergence = density * (slopes[1][0] + slopes[2][1] + slopes[3][2])
    rates = [-carried[0] - divergence]
    for j in range(3):
        rates.append(-carried[1 + j] - slopes[4][j] * inverse)
    rates.append(-carried[4] - mean[4] * mean[4] * divergence)
    return rates


def lamb(u_ref, block):
    u = [block.get(u_ref, c) * (1.0 / 12.0) for c in range(3)]
    d = [derivatives(u_ref, c, block, tuple(k for k in range(3) if k != c)) for c in range(3)]
    spin = (d[2][1] - d[1][1], d[0][1] - d[2][0], d[1][0] - d[0][0])
    return [
        spin[1] * u[2] - spin[2] * u[1],
        spin[2] * u[0] - spin[0] * u[2],
        spin[0] * u[1] - spin[1] * u[0],
    ]


def kernel(
    nx,
    nr,
    fields,
    mean_flow,
    all_blocks,
    out,
    last_slope,
    own,
    own_mean,
    own_speed,
    start,
    mean,
    speed,
    source,
    odd,
    even,
    flux,
    slope,
    send,
    receive,
    local,
    ready,
    blocks,
):
    sec = lax.axis_index("sec")
    gx = lax.axis_index("gx")
    row = lax.axis_index("row")
    is_flow = sec == 0
    is_sound = sec == 1
    first, last = gx == 0, gx == nx - 1

    def place(section, dx, dy):
        return {
            "sec": section,
            "gx": lax.rem(gx + dx + nx, nx),
            "row": lax.rem(row + dy + nr, nr),
        }

    barrier = pltpu.get_barrier_semaphore()

    def greet(device):
        pl.semaphore_signal(barrier, inc=1, device_id=device, device_id_type=MESH)

    for dx, dy in DIRECTIONS:
        greet(place(sec, dx, dy))

    @pl.when((is_sound & (gx < nx - 1)) | (is_flow & last))
    def _():
        greet(place(1 - sec, 0, 0))

    @pl.when(is_sound & first)
    def _():
        for dy in (-1, 0, 1):
            greet(place(0, -1, dy))

    @pl.when(is_sound & last)
    def _():
        for dy in (-1, 0, 1):
            greet(place(0, 1, dy))

    inner = (slice(None), pl.ds(BEGIN[0], OWN), pl.ds(BEGIN[1], OWN))
    load = pltpu.make_async_copy(fields.at[0], own, local.at[0])
    load.start()
    load_start = pltpu.make_async_copy(fields.at[0], start.at[inner], local.at[1])
    load_start.start()
    load_mean = pltpu.make_async_copy(mean_flow, own_mean, local.at[2])
    load_blocks = pltpu.make_async_copy(all_blocks, blocks, local.at[4])
    load_inner = pltpu.make_async_copy(mean_flow, mean.at[inner], local.at[3])

    @pl.when(is_sound)
    def _():
        load_mean.start()
        load_inner.start()
        load_blocks.start()

    load.wait()

    @pl.when(is_flow)
    def _():
        for x in range(OWN):
            inverse = 1.0 / own[0, x]
            for j in range(3):
                own_speed[j, x] = own[1 + j, x] * inverse

    @pl.when(is_sound)
    def _():
        load_mean.wait()

    for found, peers in (
        (is_flow & first, 12),
        (is_flow & (gx > 0) & (gx < nx - 1), 9),
        (is_flow & last, 11),
        (is_sound & (gx < nx - 1), 8),
        (is_sound & last, 9),
    ):

        @pl.when(found)
        def _():
            pl.semaphore_wait(barrier, peers)

    @pl.when(is_sound & last)
    def _():
        pl.semaphore_signal(ready, inc=1, device_id=place(0, 0, 0), device_id_type=MESH)

    def remote(origin, target, index, device):
        return pltpu.make_async_remote_copy(
            src_ref=origin,
            dst_ref=target,
            send_sem=send.at[index],
            recv_sem=receive.at[index],
            device_id=device,
            device_id_type=MESH,
        )

    def copies(section, origin, held, target, base, count=8, width=HALO):
        made = []
        for i in range(count):
            block, middle, slot = parts(DIRECTIONS[i], width)
            made.append(
                remote(
                    origin.at[middle if held else block],
                    target.at[slot],
                    base + i,
                    place(section, *DIRECTIONS[i]),
                )
            )
        return made

    field_copies = copies(sec, own, False, start, FIELD)
    mean_copies = copies(1, own_mean, False, mean, MEAN, count=4, width=2)
    speed_copies = copies(1, speed, True, speed, SPEED)
    around = copies(1, own_speed, False, speed, SPEED)
    stage_copies = copies(sec, even, True, even, STAGE)
    partner_copy = remote(own_speed, speed.at[inner], PARTNER, place(1, 0, 0))
    up = [i for i, d in enumerate(DIRECTIONS) if d[0] == 1]
    down = [i for i, d in enumerate(DIRECTIONS) if d[0] == -1]
    level = [i for i, d in enumerate(DIRECTIONS) if d[0] == 0]

    for copy in field_copies:
        copy.start()

    @pl.when(is_flow & (gx < nx - 1))
    def _():
        partner_copy.start()

    @pl.when(is_flow & first)
    def _():
        for i in down:
            around[i].start()

    @pl.when(is_flow & last)
    def _():
        for i in up:
            around[i].start()
        pl.semaphore_wait(ready, 1)
        partner_copy.start()

    @pl.when(is_sound)
    def _():
        for copy in mean_copies:
            copy.start()

    def advance(rate, prepare):
        prepare(odd, 0)

        def second(block):
            for c, k in enumerate(rate(odd, block)):
                block.put(even, c, block.get(start, c) + (0.5 * STEP_DT) * k)
                block.put(slope, c, block.get(slope, c) + 2.0 * k)

        sweep(second)
        for copy in stage_copies:
            copy.start()

        def third(block):
            for c, k in enumerate(rate(even, block)):
                block.put(odd, c, block.get(start, c) + STEP_DT * k)
                block.put(slope, c, block.get(slope, c) + 2.0 * k)

        for i in level:
            stage_copies[i].wait()
        prepare(even, 1)
        sweep_middle(third)
        for i in up + down:
            stage_copies[i].wait()
        prepare(even, 2)
        sweep_rest(third)
        prepare(odd, 0)

        def fourth(block):
            for c, k in enumerate(rate(odd, block)):
                columns = pl.ds(block.x - BEGIN[0], block.columns)
                out[0, c, columns] = block.get(start, c) + (STEP_DT / 6.0) * block.get(slope, c)
                last_slope[0, c, columns] = k

        sweep(fourth)

    load_start.wait()

    @pl.when(is_flow)
    def _():
        def rate(ref, block):
            return flow_rates(ref, flux, block)

        def prepare(ref, step):
            def columns(x, carry):
                fluxes(ref, flux, tall(x))
                return carry

            def beside(i, carry):
                fluxes(ref, flux, tall(jnp.where(i < 2, LOW - 2 + i, HIGH - 2 + i)))
                return carry

            def ends(i, carry):
                reach = 2 if step == 0 else HALO
                fluxes(ref, flux, flat(jnp.where(i == 0, LOW - reach, HIGH + reach - 2)))
                return carry

            if step < 2:
                lax.fori_loop(LOW, HIGH, columns, 0)
            if step == 2:
                lax.fori_loop(0, 4, beside, 0)
            if step != 1:
                lax.fori_loop(0, 2, ends, 0)

        def one(block):
            for c, k in enumerate(rate(start, block)):
                block.put(odd, c, block.get(start, c) + (0.5 * STEP_DT) * k)
                block.put(slope, c, k)

        for i in level:
            field_copies[i].wait_recv()
        prepare(start, 1)
        sweep_middle(one)
        for i in up + down:
            field_copies[i].wait_recv()
        prepare(start, 2)
        sweep_rest(one)
        advance(rate, prepare)
        partner_copy.wait_send()

    @pl.when(is_sound)
    def _():
        partner_copy.wait_recv()
        for i in level:
            speed_copies[i].start()

        @pl.when(gx < nx - 1)
        def _():
            for i in up:
                speed_copies[i].start()

        @pl.when(gx > 0)
        def _():
            for i in down:
                speed_copies[i].start()

        for copy in field_copies + mean_copies:
            copy.wait_recv()
        load_inner.wait()
        load_blocks.wait()

        def plain(block):
            for c, k in enumerate(sound_rates(start, mean, block)):
                block.put(slope, c, k)

        sweep_middle(plain)
        sweep_rest(plain)

        cells = nx * OWN

        def one(block):
            masks = []
            for i in range(block.columns):
                cell = lax.rem(gx * OWN + block.x + i - BEGIN[0] + cells, cells)
                masks.append(blocks[cell // MBLEN].astype(jnp.float32))
            terms = lamb(speed, block)
            for j in range(3):
                for i in range(block.columns):
                    column = Block(block.x + i, 1, block.y, block.rows)
                    column.put(source, j, masks[i] * terms[j][i : i + 1])
            for c in range(5):
                k = block.get(slope, c)
                if 1 <= c <= 3:
                    k = k - block.get(source, c - 1)
                    block.put(slope, c, k)
                block.put(odd, c, block.get(start, c) + (0.5 * STEP_DT) * k)

        for i in level:
            speed_copies[i].wait_recv()
        sweep_middle(one)
        for i in up + down:
            speed_copies[i].wait_recv()
        sweep_rest(one)

        def rate(ref, block):
            rates = sound_rates(ref, mean, block)
            return [
                k - block.get(source, c - 1) if 1 <= c <= 3 else k for c, k in enumerate(rates)
            ]

        advance(rate, lambda ref, step: None)
        for i in level:
            speed_copies[i].wait_send()

        @pl.when(gx < nx - 1)
        def _():
            for i in up:
                speed_copies[i].wait_send()

        @pl.when(gx > 0)
        def _():
            for i in down:
                speed_copies[i].wait_send()

        for copy in mean_copies:
            copy.wait_send()

    for copy in field_copies:
        copy.wait_send()

    @pl.when(is_flow & last)
    def _():
        for i in up:
            around[i].wait_send()

    @pl.when(is_flow & first)
    def _():
        for i in down:
            around[i].wait_send()


def solution(mesh):
    nx, nr = mesh.shape["gx"], mesh.shape["row"]

    def local(fields, mean_flow, source_blocks):
        fields = pltpu.with_memory_space_constraint(fields, pltpu.HBM)
        mean_flow = pltpu.with_memory_space_constraint(mean_flow, pltpu.HBM)
        source_blocks = pltpu.with_memory_space_constraint(source_blocks, pltpu.HBM)
        state, last_slope = pl.pallas_call(
            functools.partial(kernel, nx, nr),
            out_shape=[jax.ShapeDtypeStruct(fields.shape, jnp.float32)] * 2,
            in_specs=[
                pl.BlockSpec(memory_space=pltpu.HBM),
                pl.BlockSpec(memory_space=pltpu.HBM),
                pl.BlockSpec(memory_space=pltpu.HBM),
            ],
            out_specs=[pl.BlockSpec(memory_space=pltpu.VMEM)] * 2,
            scratch_shapes=[
                pltpu.VMEM((5, OWN, OWN, 128), jnp.float32),
                pltpu.VMEM((5, OWN, OWN, 128), jnp.float32),
                pltpu.VMEM((3, OWN, OWN, 128), jnp.float32),
                pltpu.VMEM((5,) + WINDOW, jnp.float32),
                pltpu.VMEM((5,) + WINDOW, jnp.float32),
                pltpu.VMEM((3,) + WINDOW, jnp.float32),
                pltpu.VMEM((3,) + WINDOW, jnp.float32),
                pltpu.VMEM((5,) + WINDOW, jnp.float32),
                pltpu.VMEM((5,) + WINDOW, jnp.float32),
                pltpu.VMEM((12,) + WINDOW, jnp.float32),
                pltpu.VMEM((5,) + WINDOW, jnp.float32),
                pltpu.SemaphoreType.DMA((SEMAPHORES,)),
                pltpu.SemaphoreType.DMA((SEMAPHORES,)),
                pltpu.SemaphoreType.DMA((5,)),
                pltpu.SemaphoreType.REGULAR,
                pltpu.SMEM(source_blocks.shape, jnp.int32),
            ],
            compiler_params=pltpu.CompilerParams(
                collective_id=0, has_side_effects=True, vmem_limit_bytes=16 * 1024 * 1024
            ),
        )(fields, mean_flow, source_blocks)
        return state + (STEP_DT / 6.0) * last_slope

    return jax.shard_map(
        local,
        mesh=mesh,
        in_specs=(P("sec", None, "gx", "row", None), P(None, "gx", "row", None), P()),
        out_specs=P("sec", None, "gx", "row", None),
        check_vma=False,
    )
```

```python
import functools

import jax
import jax.numpy as jnp
from jax import lax
from jax.experimental import pallas as pl
from jax.experimental.pallas import tpu as pltpu
from jax.sharding import PartitionSpec as P

MESH = pl.DeviceIdType.MESH
MBLEN = 4
GAMMA = 1.4
STEP_DT = 0.2
VISCOSITY = 0.05

OWN = 8
HALO = 4
BEGIN = (HALO, 8)
WINDOW = (OWN + 2 * HALO, 24, 128)

DIRECTIONS = ((1, 0), (-1, 0), (0, 1), (0, -1), (1, 1), (1, -1), (-1, 1), (-1, -1))

FIELD, SPEED, STAGE, MEAN, PARTNER = 0, 8, 16, 24, 32
SEMAPHORES = 33


def part(d, width, begin):
    if d == 1:
        return OWN - width, begin - width, width
    if d == -1:
        return 0, begin + OWN, width
    return 0, begin, OWN


def parts(direction, width):
    if direction[0] and direction[1]:
        width = 2
    both = [part(d, width, begin) for d, begin in zip(direction, BEGIN)]
    every = (slice(None),)
    return (
        every + tuple(pl.ds(s, n) for s, _, n in both),
        every + tuple(pl.ds(begin + s, n) for (s, _, n), begin in zip(both, BEGIN)),
        every + tuple(pl.ds(t, n) for _, t, n in both),
    )


def turn(values, by):
    return pltpu.roll(values, (-by) % values.shape[-1], values.ndim - 1)


class Block:
    def __init__(self, x, columns, y, rows):
        self.x, self.columns, self.y, self.rows = x, columns, y, rows

    def at(self, dx=0, dy=0):
        return (pl.ds(self.x + dx, self.columns), pl.ds(self.y + dy, self.rows))

    def get(self, ref, c, dx=0, dy=0):
        return ref[(c,) + self.at(dx, dy)]

    def put(self, ref, c, values):
        ref[(c,) + self.at()] = values


def tall(x):
    return Block(x, 1, BEGIN[1] - HALO, OWN + 2 * HALO)


def flat(x):
    return Block(x, 2, BEGIN[1], OWN)


LOW, HIGH = BEGIN[0], BEGIN[0] + OWN


def sweep(body):
    def own(i, carry):
        body(flat(LOW + 2 * i))
        return carry

    lax.fori_loop(0, OWN // 2, own, 0, unroll=2)


def sweep_middle(body):
    def middle(x, carry):
        body(tall(x))
        return carry

    lax.fori_loop(LOW + 2, HIGH - 2, middle, 0, unroll=2)


def sweep_rest(body):
    def edge(i, carry):
        body(tall(jnp.where(i < 2, LOW + i, HIGH - 4 + i)))
        return carry

    def side(i, carry):
        body(flat(jnp.where(i == 0, LOW - 2, HIGH)))
        return carry

    lax.fori_loop(0, 4, edge, 0, unroll=2)
    lax.fori_loop(0, 2, side, 0, unroll=2)


def derivatives(ref, c, block, axes=(0, 1, 2)):
    found = []
    for axis in axes:
        if axis == 2:
            value = block.get(ref, c)
            once = turn(value, 1) - turn(value, -1)
            found.append(8.0 * once - (turn(once, 1) + turn(once, -1)))
        else:
            near, far = [
                block.get(ref, c, *((by, 0) if axis == 0 else (0, by)))
                - block.get(ref, c, *((-by, 0) if axis == 0 else (0, -by)))
                for by in (1, 2)
            ]
            found.append(8.0 * near - far)
    return found


def fluxes(q_ref, f_ref, block):
    q = [block.get(q_ref, c) for c in range(5)]
    inverse = 1.0 / q[0]
    u = [q[1 + j] * inverse for j in range(3)]
    p = (GAMMA - 1.0) * (q[4] - 0.5 * (q[1] * u[0] + q[2] * u[1] + q[3] * u[2]))
    h = q[4] + p
    for d in range(3):
        for j in range(3):
            part = q[1 + j] * u[d]
            block.put(f_ref, 4 * d + j, part + p if j == d else part)
        block.put(f_ref, 4 * d + 3, h * u[d])


def flow_rates(q_ref, f_ref, block):
    rates = []
    for c in range(5):
        f = [(q_ref, 1 + d) if c == 0 else (f_ref, 4 * d + c - 1) for d in range(3)]
        sums = []
        for by in (1, 2):
            ahead, behind = ((by, 0), (0, by)), ((-by, 0), (0, -by))
            flow = [
                block.get(*f[d], *behind[d]) - block.get(*f[d], *ahead[d]) for d in range(2)
            ]
            spread = [
                block.get(q_ref, c, *ahead[d]) + block.get(q_ref, c, *behind[d]) for d in range(2)
            ]
            sums.append((flow[0] + flow[1], spread[0] + spread[1]))
        q, along = block.get(q_ref, c), block.get(*f[2])
        eight, near, far = 8.0 * along, (16.0 * VISCOSITY) * q, VISCOSITY * q
        total = 8.0 * sums[0][0] - sums[1][0] + (16.0 * VISCOSITY) * sums[0][1]
        total -= VISCOSITY * sums[1][1] + (90.0 * VISCOSITY) * q
        total += turn(near - eight, 1) + turn(near + eight, -1)
        total += turn(along - far, 2) - turn(along + far, -2)
        rates.append(total * (1.0 / 12.0))
    return rates


def sound_rates(a_ref, mean_ref, block):
    mean = [block.get(mean_ref, c) for c in range(5)]
    speed = [mean[j] * (1.0 / 12.0) for j in range(3)]
    density = mean[3] * (1.0 / 12.0)
    inverse = (1.0 / 12.0) / mean[3]
    slopes = [derivatives(a_ref, c, block) for c in range(5)]
    carried = [speed[0] * d[0] + speed[1] * d[1] + speed[2] * d[2] for d in slopes]
    divergence = density * (slopes[1][0] + slopes[2][1] + slopes[3][2])
    rates = [-carried[0] - divergence]
    for j in range(3):
        rates.append(-carried[1 + j] - slopes[4][j] * inverse)
    rates.append(-carried[4] - mean[4] * mean[4] * divergence)
    return rates


def lamb(u_ref, block):
    u = [block.get(u_ref, c) * (1.0 / 12.0) for c in range(3)]
    d = [derivatives(u_ref, c, block, tuple(k for k in range(3) if k != c)) for c in range(3)]
    spin = (d[2][1] - d[1][1], d[0][1] - d[2][0], d[1][0] - d[0][0])
    return [
        spin[1] * u[2] - spin[2] * u[1],
        spin[2] * u[0] - spin[0] * u[2],
        spin[0] * u[1] - spin[1] * u[0],
    ]


def kernel(
    nx,
    nr,
    fields,
    mean_flow,
    all_blocks,
    out,
    last_slope,
    own,
    own_mean,
    own_speed,
    start,
    mean,
    speed,
    source,
    odd,
    even,
    flux,
    slope,
    send,
    receive,
    local,
    ready,
    blocks,
):
    sec = lax.axis_index("sec")
    gx = lax.axis_index("gx")
    row = lax.axis_index("row")
    is_flow = sec == 0
    is_sound = sec == 1
    first, last = gx == 0, gx == nx - 1

    def place(section, dx, dy):
        return {
            "sec": section,
            "gx": lax.rem(gx + dx + nx, nx),
            "row": lax.rem(row + dy + nr, nr),
        }

    barrier = pltpu.get_barrier_semaphore()

    def greet(device):
        pl.semaphore_signal(barrier, inc=1, device_id=device, device_id_type=MESH)

    for dx, dy in DIRECTIONS:
        greet(place(sec, dx, dy))

    @pl.when((is_sound & (gx < nx - 1)) | (is_flow & last))
    def _():
        greet(place(1 - sec, 0, 0))

    @pl.when(is_sound & first)
    def _():
        for dy in (-1, 0, 1):
            greet(place(0, -1, dy))

    @pl.when(is_sound & last)
    def _():
        for dy in (-1, 0, 1):
            greet(place(0, 1, dy))

    inner = (slice(None), pl.ds(BEGIN[0], OWN), pl.ds(BEGIN[1], OWN))
    load = pltpu.make_async_copy(fields.at[0], own, local.at[0])
    load.start()
    load_start = pltpu.make_async_copy(fields.at[0], start.at[inner], local.at[1])
    load_start.start()
    load_mean = pltpu.make_async_copy(mean_flow, own_mean, local.at[2])
    load_blocks = pltpu.make_async_copy(all_blocks, blocks, local.at[4])
    load_inner = pltpu.make_async_copy(mean_flow, mean.at[inner], local.at[3])

    @pl.when(is_sound)
    def _():
        load_mean.start()
        load_inner.start()
        load_blocks.start()

    load.wait()

    @pl.when(is_flow)
    def _():
        for x in range(OWN):
            inverse = 1.0 / own[0, x]
            for j in range(3):
                own_speed[j, x] = own[1 + j, x] * inverse

    @pl.when(is_sound)
    def _():
        load_mean.wait()

    for found, peers in (
        (is_flow & first, 12),
        (is_flow & (gx > 0) & (gx < nx - 1), 9),
        (is_flow & last, 11),
        (is_sound & (gx < nx - 1), 8),
        (is_sound & last, 9),
    ):

        @pl.when(found)
        def _():
            pl.semaphore_wait(barrier, peers)

    @pl.when(is_sound & last)
    def _():
        pl.semaphore_signal(ready, inc=1, device_id=place(0, 0, 0), device_id_type=MESH)

    def remote(origin, target, index, device):
        return pltpu.make_async_remote_copy(
            src_ref=origin,
            dst_ref=target,
            send_sem=send.at[index],
            recv_sem=receive.at[index],
            device_id=device,
            device_id_type=MESH,
        )

    def copies(section, origin, held, target, base, count=8, width=HALO):
        made = []
        for i in range(count):
            block, middle, slot = parts(DIRECTIONS[i], width)
            made.append(
                remote(
                    origin.at[middle if held else block],
                    target.at[slot],
                    base + i,
                    place(section, *DIRECTIONS[i]),
                )
            )
        return made

    field_copies = copies(sec, own, False, start, FIELD)
    mean_copies = copies(1, own_mean, False, mean, MEAN, count=4, width=2)
    speed_copies = copies(1, speed, True, speed, SPEED)
    around = copies(1, own_speed, False, speed, SPEED)
    stage_copies = copies(sec, even, True, even, STAGE)
    partner_copy = remote(own_speed, speed.at[inner], PARTNER, place(1, 0, 0))
    up = [i for i, d in enumerate(DIRECTIONS) if d[0] == 1]
    down = [i for i, d in enumerate(DIRECTIONS) if d[0] == -1]
    level = [i for i, d in enumerate(DIRECTIONS) if d[0] == 0]

    for copy in field_copies:
        copy.start()

    @pl.when(is_flow & (gx < nx - 1))
    def _():
        partner_copy.start()

    @pl.when(is_flow & first)
    def _():
        for i in down:
            around[i].start()

    @pl.when(is_flow & last)
    def _():
        for i in up:
            around[i].start()
        pl.semaphore_wait(ready, 1)
        partner_copy.start()

    @pl.when(is_sound)
    def _():
        for copy in mean_copies:
            copy.start()

    def advance(rate, prepare):
        prepare(odd, 0)

        def second(block):
            for c, k in enumerate(rate(odd, block)):
                block.put(even, c, block.get(start, c) + (0.5 * STEP_DT) * k)
                block.put(slope, c, block.get(slope, c) + 2.0 * k)

        sweep(second)
        for copy in stage_copies:
            copy.start()

        def third(block):
            for c, k in enumerate(rate(even, block)):
                block.put(odd, c, block.get(start, c) + STEP_DT * k)
                block.put(slope, c, block.get(slope, c) + 2.0 * k)

        for i in level:
            stage_copies[i].wait()
        prepare(even, 1)
        sweep_middle(third)
        for i in up + down:
            stage_copies[i].wait()
        prepare(even, 2)
        sweep_rest(third)
        prepare(odd, 0)

        def fourth(block):
            for c, k in enumerate(rate(odd, block)):
                columns = pl.ds(block.x - BEGIN[0], block.columns)
                out[0, c, columns] = block.get(start, c) + (STEP_DT / 6.0) * block.get(slope, c)
                last_slope[0, c, columns] = k

        sweep(fourth)

    load_start.wait()

    @pl.when(is_flow)
    def _():
        def rate(ref, block):
            return flow_rates(ref, flux, block)

        def prepare(ref, step):
            def columns(x, carry):
                fluxes(ref, flux, tall(x))
                return carry

            def beside(i, carry):
                fluxes(ref, flux, tall(jnp.where(i < 2, LOW - 2 + i, HIGH - 2 + i)))
                return carry

            def ends(i, carry):
                reach = 2 if step == 0 else HALO
                fluxes(ref, flux, flat(jnp.where(i == 0, LOW - reach, HIGH + reach - 2)))
                return carry

            if step < 2:
                lax.fori_loop(LOW, HIGH, columns, 0, unroll=2)
            if step == 2:
                lax.fori_loop(0, 4, beside, 0, unroll=2)
            if step != 1:
                lax.fori_loop(0, 2, ends, 0, unroll=2)

        def one(block):
            for c, k in enumerate(rate(start, block)):
                block.put(odd, c, block.get(start, c) + (0.5 * STEP_DT) * k)
                block.put(slope, c, k)

        for i in level:
            field_copies[i].wait_recv()
        prepare(start, 1)
        sweep_middle(one)
        for i in up + down:
            field_copies[i].wait_recv()
        prepare(start, 2)
        sweep_rest(one)
        advance(rate, prepare)
        partner_copy.wait_send()

    @pl.when(is_sound)
    def _():
        partner_copy.wait_recv()

        @pl.when(gx < nx - 1)
        def _():
            for i in up:
                speed_copies[i].start()

        @pl.when(gx > 0)
        def _():
            for i in down:
                speed_copies[i].start()

        for i in level:
            speed_copies[i].start()

        for copy in field_copies + mean_copies:
            copy.wait_recv()
        load_inner.wait()
        load_blocks.wait()

        def plain(block):
            for c, k in enumerate(sound_rates(start, mean, block)):
                block.put(slope, c, k)

        sweep_middle(plain)
        sweep_rest(plain)

        cells = nx * OWN

        def one(block):
            masks = []
            for i in range(block.columns):
                cell = lax.rem(gx * OWN + block.x + i - BEGIN[0] + cells, cells)
                masks.append(blocks[cell // MBLEN].astype(jnp.float32))
            terms = lamb(speed, block)
            for j in range(3):
                for i in range(block.columns):
                    column = Block(block.x + i, 1, block.y, block.rows)
                    column.put(source, j, masks[i] * terms[j][i : i + 1])
            for c in range(5):
                k = block.get(slope, c)
                if 1 <= c <= 3:
                    k = k - block.get(source, c - 1)
                    block.put(slope, c, k)
                block.put(odd, c, block.get(start, c) + (0.5 * STEP_DT) * k)

        for i in level:
            speed_copies[i].wait_recv()
        sweep_middle(one)
        for i in up + down:
            speed_copies[i].wait_recv()
        sweep_rest(one)

        def rate(ref, block):
            rates = sound_rates(ref, mean, block)
            return [
                k - block.get(source, c - 1) if 1 <= c <= 3 else k for c, k in enumerate(rates)
            ]

        advance(rate, lambda ref, step: None)
        for i in level:
            speed_copies[i].wait_send()

        @pl.when(gx < nx - 1)
        def _():
            for i in up:
                speed_copies[i].wait_send()

        @pl.when(gx > 0)
        def _():
            for i in down:
                speed_copies[i].wait_send()

        for copy in mean_copies:
            copy.wait_send()

    for copy in field_copies:
        copy.wait_send()

    @pl.when(is_flow & last)
    def _():
        for i in up:
            around[i].wait_send()

    @pl.when(is_flow & first)
    def _():
        for i in down:
            around[i].wait_send()


def solution(mesh):
    nx, nr = mesh.shape["gx"], mesh.shape["row"]

    def local(fields, mean_flow, source_blocks):
        fields = pltpu.with_memory_space_constraint(fields, pltpu.HBM)
        mean_flow = pltpu.with_memory_space_constraint(mean_flow, pltpu.HBM)
        source_blocks = pltpu.with_memory_space_constraint(source_blocks, pltpu.HBM)
        state, last_slope = pl.pallas_call(
            functools.partial(kernel, nx, nr),
            out_shape=[jax.ShapeDtypeStruct(fields.shape, jnp.float32)] * 2,
            in_specs=[
                pl.BlockSpec(memory_space=pltpu.HBM),
                pl.BlockSpec(memory_space=pltpu.HBM),
                pl.BlockSpec(memory_space=pltpu.HBM),
            ],
            out_specs=[pl.BlockSpec(memory_space=pltpu.VMEM)] * 2,
            scratch_shapes=[
                pltpu.VMEM((5, OWN, OWN, 128), jnp.float32),
                pltpu.VMEM((5, OWN, OWN, 128), jnp.float32),
                pltpu.VMEM((3, OWN, OWN, 128), jnp.float32),
                pltpu.VMEM((5,) + WINDOW, jnp.float32),
                pltpu.VMEM((5,) + WINDOW, jnp.float32),
                pltpu.VMEM((3,) + WINDOW, jnp.float32),
                pltpu.VMEM((3,) + WINDOW, jnp.float32),
                pltpu.VMEM((5,) + WINDOW, jnp.float32),
                pltpu.VMEM((5,) + WINDOW, jnp.float32),
                pltpu.VMEM((12,) + WINDOW, jnp.float32),
                pltpu.VMEM((5,) + WINDOW, jnp.float32),
                pltpu.SemaphoreType.DMA((SEMAPHORES,)),
                pltpu.SemaphoreType.DMA((SEMAPHORES,)),
                pltpu.SemaphoreType.DMA((5,)),
                pltpu.SemaphoreType.REGULAR,
                pltpu.SMEM(source_blocks.shape, jnp.int32),
            ],
            compiler_params=pltpu.CompilerParams(
                collective_id=0, has_side_effects=True, vmem_limit_bytes=16 * 1024 * 1024
            ),
        )(fields, mean_flow, source_blocks)
        return state + (STEP_DT / 6.0) * last_slope

    return jax.shard_map(
        local,
        mesh=mesh,
        in_specs=(P("sec", None, "gx", "row", None), P(None, "gx", "row", None), P()),
        out_specs=P("sec", None, "gx", "row", None),
        check_vma=False,
    )
```
